128 devices in a mesh: row: 16 (over y, z), col: 8 (over x, core).
Axes of the slice: x: 4, y: 4, z: 4, core: 2. Of those that a mesh axis runs over, the one named last changes fastest.
Arguments:
- fock_matrix: bfloat16 [3072, 3072], P('row', 'col'), as said below
- density: bfloat16 [3072, 3072], P('row', 'col'), as said below
- margin: bfloat16 [3072, 3072], P('row', 'col'), as said below
- fill_patterns: int32 [3, 96, 96], P(None, 'row', 'col'), may hold values from 0 to 1, as said below
- first_filters: int32 [3, 96, 96], P(None, 'row', 'col'), may hold values from 0 to 1, as said below
- owner_order: int32 [96], replicated, may hold values from 0 to 95, as said below
- second_filters: int32 [7, 96, 96], P(None, 'row', 'col'), may hold values from 0 to 1, as said below
Outputs:
- evolved: bfloat16 [3072, 3072], P('row', 'col')
The draws below stay inside these ranges and needn't reach their ends.
Inputs may be any that keep to these rules, and one draw needn't show every extreme that they name: `fock_matrix`: Symmetric. `density`: Symmetric. `margin`: Symmetric, with unit diagonal. `fill_patterns`: each entry says whether a block is kept; each pattern is symmetric and keeps every diagonal block. `first_filters`: each entry says whether a block of the product is kept; each filter is symmetric and keeps every diagonal block. `second_filters`: each entry says whether a block of the product is kept, indexed in owner order; each filter is symmetric and keeps every diagonal block. `owner_order`: A permutation of the 96 block indices.
All inputs are finite; a program needn't handle non-finite values.
Results may differ from the reference program's by a relative error of at most 0.012.
Values may be sent and summed in bfloat16 or wider, within the bound.
A program may use at most 64 MiB of HBM per device.

```python
import jax
import jax.numpy as jnp

BLK = 32
PANEL = 6
TERMS = 6
SQUARINGS = 2
NB = 96
N = 3072


def pattern(key, variant, layers):
    weights = jax.random.randint(jax.random.fold_in(key, 11), (NB,), 1, 9)
    threshold = weights[:, None] * weights[None, :]
    rolled = jax.random.randint(jax.random.fold_in(key, variant), (layers, NB, NB), 0, 96)
    retained = (rolled < threshold[None]).astype(jnp.int32)
    retained = jnp.maximum(retained, jnp.swapaxes(retained, 1, 2))
    diagonal = (jnp.arange(NB)[:, None] == jnp.arange(NB)[None, :]).astype(jnp.int32)
    return jnp.maximum(retained, diagonal[None])


def symmetric(key, scale):
    raw = jax.random.normal(key, (N, N), jnp.float32)
    return (raw + raw.T) * (0.70710678 * scale)


def draw_fock_matrix(key, part):
    return symmetric(jax.random.fold_in(key, 31), 11.0 / N).astype(jnp.bfloat16)


def draw_density(key, part):
    return symmetric(jax.random.fold_in(key, 32), 1.0).astype(jnp.bfloat16)


def draw_margin(key, part):
    off = symmetric(jax.random.fold_in(key, 33), 0.35 / N ** 0.5)
    unit = (jnp.arange(N)[:, None] == jnp.arange(N)[None, :]).astype(jnp.float32)
    return (off * (1.0 - unit) + unit).astype(jnp.bfloat16)


def draw_fill_patterns(key, part):
    return pattern(key, 21, 3)


def draw_first_filters(key, part):
    return pattern(key, 22, 3)


def draw_second_filters(key, part):
    return pattern(key, 23, TERMS - 1 + SQUARINGS)


def place_value(order, position, target):
    located = jnp.argmax(order == target).astype(jnp.int32)
    former = order[position]
    order = order.at[located].set(former)
    return order.at[position].set(target)


def draw_owner_order(key, part):
    order = jax.random.permutation(jax.random.fold_in(key, 41), NB).astype(jnp.int32)
    anchor = jax.random.randint(jax.random.fold_in(key, 42), (), 0, NB).astype(jnp.int32)
    order = place_value(order, anchor, (anchor - PANEL) % NB)
    opposite = (anchor + NB // 2) % NB
    order = place_value(order, opposite, anchor)
    following = (anchor + PANEL) % NB
    order = place_value(order, following, (anchor + 2 * PANEL) % NB)
    return order


def setup_inputs(seed: int = 0) -> dict:
    keys = jax.random.split(jax.random.key(seed), 8)
    return {
        "fock_matrix": draw_fock_matrix(jax.random.fold_in(keys[7], 71), 0),
        "density": draw_density(jax.random.fold_in(keys[7], 71), 0),
        "margin": draw_margin(jax.random.fold_in(keys[7], 71), 0),
        "fill_patterns": draw_fill_patterns(jax.random.fold_in(keys[7], 71), 0),
        "first_filters": draw_first_filters(jax.random.fold_in(keys[7], 71), 0),
        "owner_order": draw_owner_order(jax.random.fold_in(keys[7], 71), 0),
        "second_filters": draw_second_filters(jax.random.fold_in(keys[7], 71), 0),
    }


def expand(mask, values):
    row_blocks = mask.shape[0]
    column_blocks = mask.shape[1]
    block_size = values.shape[0] // row_blocks
    shaped = values.reshape(row_blocks, block_size, column_blocks, block_size) * mask[:, None, :, None].astype(values.dtype)
    return shaped.reshape(values.shape)


def product(former, latter):
    return jnp.dot(former, latter, preferred_element_type=jnp.float32)


def reference(fock_matrix, density, margin, fill_patterns, first_filters, owner_order, second_filters):
    masked_fock = expand(fill_patterns[0], fock_matrix)
    masked_density = expand(fill_patterns[1], density)
    masked_margin = expand(fill_patterns[2], margin)
    fock_density = expand(first_filters[0], product(masked_fock, masked_density)).astype(jnp.bfloat16)
    margin_density = expand(first_filters[1], product(masked_margin, masked_density)).astype(jnp.bfloat16)
    generator = product(fock_density, masked_margin) - product(margin_density, masked_fock)
    generator = expand(first_filters[2], generator).astype(jnp.bfloat16)
    blocks = generator.reshape(NB, BLK, NB, BLK)
    reordered = jnp.take(jnp.take(blocks, owner_order, axis=0), owner_order, axis=2).reshape(N, N)
    scaled = (reordered.astype(jnp.float32) * 0.25).astype(jnp.bfloat16)
    identity = jnp.eye(N, dtype=jnp.float32)
    series = (identity + scaled.astype(jnp.float32) / 6.0).astype(jnp.bfloat16)
    for number in range(TERMS - 1):
        degree = TERMS - 1 - number
        series = (identity + expand(second_filters[number], product(scaled, series)) / degree).astype(jnp.bfloat16)
    for number in range(SQUARINGS):
        series = expand(second_filters[TERMS - 1 + number], product(series, series)).astype(jnp.bfloat16)
    return series
```

```python
import jax
import jax.numpy as jnp
from jax import lax
from jax.experimental import pallas as pl
from jax.experimental.pallas import tpu as pltpu
from jax.sharding import PartitionSpec as P

MESH = pl.DeviceIdType.MESH
BLK = 32
TERMS = 6
RB = 6
CB = 12
TR = 192
TC = 384
N = 3072
NB = 96
SEMS = 320
BF = jnp.bfloat16
F32 = jnp.float32


def iota(shape, axis):
    return lax.broadcasted_iota(jnp.int32, shape, axis)


def mm(a, b):
    return jnp.dot(a, b, preferred_element_type=F32)


class Net:
    def __init__(self, send, recv):
        self.send, self.recv, self.used, self.copies = send, recv, 0, []

    def copy(self, src, dst, device):
        number = self.used
        self.used += 1
        made = pltpu.make_async_remote_copy(
            src, dst, self.send.at[number], self.recv.at[number], device_id=device, device_id_type=MESH
        )
        self.copies.append(made)
        return made

    def finish(self):
        for made in self.copies:
            made.wait_send()


class Ring:
    def __init__(self, net, k, after, before, piece):
        self.net = net
        p = lambda step, part: piece(lax.rem(k + step + 4, 4), part)
        c = lambda ref, device: net.copy(ref, ref, device)
        self.a0, self.b1 = c(p(0, 0), after), c(p(0, 1), before)
        self.a1, self.b0 = c(p(0, 1), after), c(p(0, 0), before)
        self.f0, self.f1 = c(p(-1, 0), after), c(p(1, 1), before)

    def start(self):
        for made in (self.a0, self.b1, self.a1, self.b0):
            made.start()

    def forward(self):
        self.a0.wait_recv()
        self.f0.start()
        self.b1.wait_recv()
        self.f1.start()

    def near(self):
        self.a1.wait_recv()
        self.b0.wait_recv()

    def far(self):
        self.f0.wait_recv()
        self.f1.wait_recv()


def body(
    fock, density, margin, fills, firsts, seconds, order_s, order_v, out,
    colp, cols_, colf, coly, colt, colz, blocks, rows, acc, masks, fl, xs, xr, send, recv, local,
):
    r, c = lax.axis_index("row"), lax.axis_index("col")
    y, z = r // 4, lax.rem(r, 4)
    x, core = c // 2, lax.rem(c, 2)
    net = Net(send, recv)

    def dev(yy, zz, xx, cc):
        return (lax.rem(yy + 4, 4) * 4 + lax.rem(zz + 4, 4), lax.rem(xx + 4, 4) * 2 + cc)

    yp, ym = dev(y + 1, z, x, core), dev(y - 1, z, x, core)
    zp, zm = dev(y, z + 1, x, core), dev(y, z - 1, x, core)
    xp, xm = dev(y, z, x + 1, core), dev(y, z, x - 1, core)
    sibling = (r, 2 * x + 1 - core)
    partners = [(2 * c + h, r // 2) for h in range(2)]
    itself = [jnp.logical_and(2 * c + h == r, r // 2 == c) for h in range(2)]

    barrier = pltpu.get_barrier_semaphore()
    others = [(r, lax.rem(c + k, 8)) for k in range(1, 8)]
    for device in others + [yp, ym, zp, zm]:
        pl.semaphore_signal(barrier, inc=1, device_id=device, device_id_type=MESH)
    for h in range(2):

        @pl.when(jnp.logical_not(itself[h]))
        def _():
            pl.semaphore_signal(barrier, inc=1, device_id=partners[h], device_id_type=MESH)

    pl.semaphore_wait(barrier, 13 - jnp.where(c == r // 2, 1, 0))

    class Columns:
        def __init__(self, buf):
            self.first = (
                Ring(net, z, zp, zm, lambda k, p: buf.at[y, k, pl.ds(48 * p, 48), :]),
                Ring(net, y, yp, ym, lambda k, p: buf.at[k, z, pl.ds(96 + 48 * p, 48), :]),
            )
            self.second = (
                Ring(net, y, yp, ym, lambda k, p: buf.at[k, :, pl.ds(48 * p, 48), :]),
                Ring(net, z, zp, zm, lambda k, p: buf.at[:, k, pl.ds(96 + 48 * p, 48), :]),
            )

        def s1(self):
            for ring in self.first:
                ring.start()

        def s1f(self):
            for ring in self.first:
                ring.forward()

        def s2(self):
            for ring in self.first:
                ring.near()
                ring.far()
                ring_number = self.first.index(ring)
                self.second[ring_number].start()

        def s2f(self):
            for ring in self.second:
                ring.forward()

        def done(self):
            for ring in self.second:
                ring.near()
                ring.far()

        def all(self):
            self.s1()
            self.s1f()
            self.s2()
            self.s2f()
            self.done()

    class Rows:
        def __init__(self, number):
            piece = lambda k, p: rows.at[number, pl.ds(96 * p, 96), pl.ds((2 * k + core) * TC, TC)]
            self.ring = Ring(net, x, xp, xm, piece)
            self.pairs = []
            for step in (0, -1, 1, 2):
                k = lax.rem(x + step + 4, 4)
                ref = rows.at[number, :, pl.ds((2 * k + core) * TC, TC)]
                self.pairs.append(net.copy(ref, ref, sibling))

        def start(self):
            self.ring.start()
            self.pairs[0].start()

        def forward(self):
            self.ring.forward()

        def near(self):
            self.ring.near()
            self.pairs[1].start()
            self.pairs[2].start()

        def far(self):
            self.ring.far()
            self.pairs[3].start()

        def done(self):
            for made in self.pairs:
                made.wait_recv()

        def all(self):
            self.start()
            self.forward()
            self.near()
            self.far()
            self.done()

    spread_rows = (iota((TR, RB), 0) // BLK == iota((TR, RB), 1)).astype(BF)
    spread_cols = (iota((CB, TC), 0) == iota((CB, TC), 1) // BLK).astype(BF)

    def expand(mask):
        wide = mm(mask.astype(F32).astype(BF), spread_cols).astype(BF)
        return mm(spread_rows, wide)

    def own(number):
        return rows.at[number, :, pl.ds(pl.multiple_of(c * TC, TC), TC)]

    def product(number, buf, start=None, sign=1.0):
        acc[...] = jnp.zeros_like(acc) if start is None else start

        @pl.loop(0, 4)
        def _(k):
            left = rows[number, :, pl.ds(pl.multiple_of(k * 768, 768), 768)]
            acc[...] += sign * mm(left, buf[k].reshape(768, TC))

    shift = (iota((CB, 128), 1) == c * CB + iota((CB, 128), 0)).astype(BF)
    pad8 = (iota((8, RB), 0) == iota((8, RB), 1)).astype(BF)
    for number in range(TERMS - 1):
        wide = mm(seconds[number].astype(F32).astype(BF), shift).astype(BF)
        fl[c, number] = mm(pad8, wide)

    get_p, get_s, get_f = Columns(colp), Columns(cols_), Columns(colf)
    row_f, row_s, row_g, row_h = Rows(0), Rows(1), Rows(2), Rows(3)

    colp[y, z] = (density[...].astype(F32) * expand(fills[1])).astype(BF)
    get_p.s1()
    masked = (fock[...].astype(F32) * expand(fills[0])).astype(BF)
    own(0)[...] = masked
    colf[y, z] = masked
    row_f.start()
    masked = (margin[...].astype(F32) * expand(fills[2])).astype(BF)
    own(1)[...] = masked
    cols_[y, z] = masked
    row_s.start()
    filters = []
    for device in others:
        made = net.copy(fl.at[c], fl.at[c], device)
        made.start()
        filters.append(made)
    get_p.s1f()
    row_f.forward()
    get_p.s2()
    row_f.near()
    for number in range(3):
        masks[number] = expand(firsts[number]).astype(BF)
    row_s.forward()
    row_f.far()
    get_p.s2f()
    get_s.s1()
    row_s.near()
    row_s.far()
    row_f.done()
    get_p.done()
    get_s.s1f()
    product(0, colp)
    own(2)[...] = (acc[...] * masks[0].astype(F32)).astype(BF)
    row_g.start()
    row_s.done()
    get_s.s2()
    product(1, colp)
    own(3)[...] = (acc[...] * masks[1].astype(F32)).astype(BF)
    row_h.start()
    row_g.forward()
    row_g.near()
    row_h.forward()
    get_s.s2f()
    get_f.s1()
    row_g.far()
    row_h.near()
    row_h.far()
    row_g.done()
    row_h.done()
    for made in filters:
        made.wait_recv()

    total = fl[0]
    for number in range(1, 8):
        total = total + fl[number]
    spread8 = (iota((TR, 8), 0) // BLK == iota((TR, 8), 1)).astype(BF)
    place = (order_v[...] == c * CB + iota((128, TC), 1) // BLK).astype(BF)
    for number in range(TERMS - 1):
        wide = mm(total[number].astype(BF), place).astype(BF)
        masks[3 + number] = mm(spread8, wide).astype(BF)
    mine = (iota((8, 128), 1) == r * RB + iota((8, 128), 0)).astype(BF)
    wide = mm(mine, place).astype(BF)
    same = lax.rem(iota((TR, TC), 0), BLK) == lax.rem(iota((TR, TC), 1), BLK)
    masks[8] = jnp.where(same, mm(spread8, wide), 0.0).astype(BF)
    masks[9] = expand(seconds[TERMS - 1]).astype(BF)
    masks[10] = expand(seconds[TERMS]).astype(BF)

    get_s.done()
    get_f.s1f()
    product(2, cols_)
    get_f.s2()
    get_f.s2f()
    get_f.done()

    @pl.loop(0, 4)
    def _(k):
        left = rows[3, :, pl.ds(pl.multiple_of(k * 768, 768), 768)]
        acc[...] -= mm(left, colf[k].reshape(768, TC))

    def exchange(number, tile):
        turned = tile.T.astype(BF)
        made = []
        for h in range(2):
            xs[number, h] = turned[TR * h : TR * (h + 1), :]
        for h in range(2):
            copy = pltpu.make_async_remote_copy(
                xs.at[number, h], xr.at[number, lax.rem(r, 2)], send.at[SEMS - 4 + 2 * number + h],
                recv.at[SEMS - 4 + 2 * number + lax.rem(r, 2)], device_id=partners[h], device_id_type=MESH,
            )
            here = pltpu.make_async_copy(xs.at[number, h], xr.at[number, h], local.at[number])
            made.append((copy, here))

            @pl.when(itself[h])
            def _():
                here.start()

            @pl.when(jnp.logical_not(itself[h]))
            def _():
                copy.start()

        value = None
        for h in range(2):
            copy, here = made[h]
            arrival = pltpu.make_async_remote_copy(
                xs.at[number, h], xr.at[number, h], send.at[SEMS - 4 + 2 * number + h],
                recv.at[SEMS - 4 + 2 * number + h], device_id=partners[h], device_id_type=MESH,
            )

            @pl.when(itself[h])
            def _():
                here.wait()

            @pl.when(jnp.logical_not(itself[h]))
            def _():
                arrival.wait_recv()
                copy.wait_send()

            lane = (iota((TR, TC), 0) + TR * h == iota((TR, TC), 1)).astype(BF)
            part = mm(xr[number, h], lane)
            value = part if value is None else value + part
        return value

    tile = (acc[...] * masks[2].astype(F32)).astype(BF)
    turned = exchange(0, tile.astype(F32))
    coly[y, z] = (turned * 0.25).astype(BF)
    Columns(coly).all()

    def by_blocks(buf):
        @pl.loop(0, 4)
        def _(k):
            blocks[pl.ds(24 * k, 24)] = buf[k].reshape(24, BLK, TC)

    by_blocks(coly)
    for b in range(RB):
        part = blocks[order_s[r * RB + b]].astype(F32)
        own(4)[pl.ds(BLK * b, BLK), :] = (masks[8, pl.ds(BLK * b, BLK), :].astype(F32) + part / 6.0).astype(BF)
    for number in range(TERMS - 1):
        Rows(4 + number).all()
        product(4 + number, coly)
        filtered = acc[...] * masks[3 + number].astype(F32)
        value = masks[8].astype(F32) + filtered / float(TERMS - 1 - number)
        if number < TERMS - 2:
            own(5 + number)[...] = value.astype(BF)

    turned = exchange(1, value.astype(BF).astype(F32))
    colt[y, z] = turned.astype(BF)
    Columns(colt).all()
    by_blocks(colt)
    for b in range(RB):
        own(9)[pl.ds(BLK * b, BLK), :] = blocks[order_s[r * RB + b]]
    row_t = Rows(9)
    row_t.start()
    row_t.forward()
    row_t.near()
    row_t.far()
    row_t.done()
    acc[...] = jnp.zeros_like(acc)

    @pl.loop(0, 4)
    def _(k):
        left = rows[9, :, pl.ds(pl.multiple_of(k * 768, 768), 768)]
        right = jnp.concatenate([blocks[order_s[24 * k + b]] for b in range(24)], axis=0)
        acc[...] += mm(left, right)

    value = (acc[...] * masks[9].astype(F32)).astype(BF)
    own(10)[...] = value
    colz[y, z] = value
    row_z, get_z = Rows(10), Columns(colz)
    get_z.s1()
    row_z.start()
    get_z.s1f()
    row_z.forward()
    get_z.s2()
    row_z.near()
    row_z.far()
    row_z.done()
    get_z.s2f()
    get_z.done()
    product(10, colz)
    out[...] = (acc[...] * masks[10].astype(F32)).astype(BF)
    net.finish()
    assert net.used <= SEMS - 4


def on_device(fock, density, margin, fills, firsts, owner_order, seconds):
    vmem = pl.BlockSpec(memory_space=pltpu.VMEM)
    order_v = jnp.pad(owner_order, (0, 128 - owner_order.shape[0]), constant_values=-1)[:, None]
    panel = pltpu.VMEM((4, 4, TR, TC), BF)
    return pl.pallas_call(
        body,
        out_shape=jax.ShapeDtypeStruct((TR, TC), BF),
        in_specs=[vmem] * 6 + [pl.BlockSpec(memory_space=pltpu.SMEM), vmem],
        out_specs=vmem,
        scratch_shapes=[panel] * 6
        + [
            pltpu.VMEM((NB, BLK, TC), BF),
            pltpu.VMEM((11, TR, N), BF),
            pltpu.VMEM((TR, TC), F32),
            pltpu.VMEM((11, TR, TC), BF),
            pltpu.VMEM((8, TERMS - 1, 8, 128), F32),
            pltpu.VMEM((2, 2, TR, TR), BF),
            pltpu.VMEM((2, 2, TR, TR), BF),
            pltpu.SemaphoreType.DMA((SEMS,)),
            pltpu.SemaphoreType.DMA((SEMS,)),
            pltpu.SemaphoreType.DMA((2,)),
        ],
        compiler_params=pltpu.CompilerParams(
            collective_id=0, has_side_effects=True, vmem_limit_bytes=60 * 1024 * 1024
        ),
    )(fock, density, margin, fills, firsts, seconds, owner_order, order_v)


def solution(mesh):
    return jax.shard_map(
        on_device,
        mesh=mesh,
        in_specs=(
            P("row", "col"),
            P("row", "col"),
            P("row", "col"),
            P(None, "row", "col"),
            P(None, "row", "col"),
            P(),
            P(None, "row", "col"),
        ),
        out_specs=P("row", "col"),
        check_vma=False,
    )
```

```python
import jax
import jax.numpy as jnp
from jax import lax
from jax.experimental import pallas as pl
from jax.experimental.pallas import tpu as pltpu
from jax.sharding import PartitionSpec as P

MESH = pl.DeviceIdType.MESH
BLK = 32
TERMS = 6
RB = 6
CB = 12
TR = 192
TC = 384
N = 3072
NB = 96
SEMS = 336
BF = jnp.bfloat16
F32 = jnp.float32


def iota(shape, axis):
    return lax.broadcasted_iota(jnp.int32, shape, axis)


def mm(a, b):
    return jnp.dot(a, b, preferred_element_type=F32)


class Net:
    def __init__(self, sems, units):
        self.sems, self.units, self.used, self.groups = sems, units, 0, []

    def sem(self):
        self.used += 1
        return self.sems.at[self.used - 1]

    def group(self):
        made = [self.sem(), 0]
        return made

    def senders(self):
        made = self.group()
        self.groups.append(made)
        return made

    def copy(self, ref, device, sent, size, got=None, target=None):
        if got is None:
            got = self.sem()
        elif isinstance(got, list):
            got[1] += size
            got = got[0]
        sent[1] += size
        return pltpu.make_async_remote_copy(
            ref, ref if target is None else target, sent[0], got, device_id=device, device_id_type=MESH
        )

    def wait(self, group):
        ref = self.units.at[pl.ds(0, group[1])]
        pltpu.make_async_copy(ref, ref, group[0]).wait()

    def finish(self):
        for made in self.groups:
            self.wait(made)


class Ring:
    def __init__(self, net, k, nexts, piece, sizes, sent, near=None, far=None):
        after, before = nexts
        p = lambda step, part: piece(lax.rem(k + step + 4, 4), part)
        c = lambda step, part, device, got=None: net.copy(p(step, part), device, sent, sizes[part], got)
        self.a0, self.b1 = c(0, 0, after), c(0, 1, before)
        self.a1, self.b0 = c(0, 1, after, near), c(0, 0, before, near)
        self.f0, self.f1 = c(-1, 0, after, far), c(1, 1, before, far)

    def start(self):
        for made in (self.a0, self.b1, self.a1, self.b0):
            made.start()

    def forward(self):
        self.a0.wait_recv()
        self.f0.start()
        self.b1.wait_recv()
        self.f1.start()

    def near(self):
        self.a1.wait_recv()
        self.b0.wait_recv()

    def far(self):
        self.f0.wait_recv()
        self.f1.wait_recv()


class Plane:
    def __init__(self, net, k1, next1, k2, next2, piece_a, piece_b, sizes_a, sizes_b):
        self.net = net
        sends = [net.senders(), net.senders()]
        turn = lambda k, s: lax.rem(k + s + 4, 4)
        steps = (0, -1, 1, 2)
        self.ends = []

        def second(k, nexts, piece, sizes, sent):
            rings = []
            for s in steps:
                end = net.group()
                self.ends.append(end)
                rings.append(Ring(net, k, nexts, piece(s), sizes, sent, end, end))
            return rings

        self.a1 = Ring(net, k1, next1, lambda k, p: piece_a(k, k2, p), sizes_a, sends[0])
        self.a2 = second(k2, next2, lambda s: lambda k, p: piece_a(turn(k1, s), k, p), sizes_a, sends[0])
        self.b1 = Ring(net, k2, next2, lambda k, p: piece_b(k1, k, p), sizes_b, sends[1])
        self.b2 = second(k1, next1, lambda s: lambda k, p: piece_b(k, turn(k2, s), p), sizes_b, sends[1])

    def s1(self):
        self.a1.start()
        self.b1.start()
        self.a2[0].start()
        self.b2[0].start()

    def s2(self):
        self.a1.forward()
        self.b1.forward()
        for first, rings in ((self.a1, self.a2), (self.b1, self.b2)):
            first.near()
            rings[1].start()
            rings[2].start()

    def s3(self):
        self.a2[0].forward()
        self.b2[0].forward()
        for first, rings in ((self.a1, self.a2), (self.b1, self.b2)):
            first.far()
            rings[3].start()

    def s4(self):
        for number in (1, 2, 3):
            self.a2[number].forward()
            self.b2[number].forward()

    def end(self, number):
        self.net.wait(self.ends[number])

    def done(self):
        for number in range(8):
            self.end(number)


def body(
    fock, density, margin, fills, firsts, seconds, order, out,
    colp, cols_, colf, colt, colz, panel, series, units, rows, acc, masks, filters, place, turned, arrived, sems,
):
    r, c = lax.axis_index("row"), lax.axis_index("col")
    y, z = r // 4, lax.rem(r, 4)
    x, core = c // 2, lax.rem(c, 2)
    net = Net(sems, units)

    def dev(yy, zz, xx):
        return (lax.rem(yy + 4, 4) * 4 + lax.rem(zz + 4, 4), lax.rem(xx + 4, 4) * 2 + core)

    next_y = (dev(y + 1, z, x), dev(y - 1, z, x))
    next_z = (dev(y, z + 1, x), dev(y, z - 1, x))
    next_x = (dev(y, z, x + 1), dev(y, z, x - 1))
    across = dev(y, z + 2, x)
    sibling = (r, 2 * x + 1 - core)

    barrier = pltpu.get_barrier_semaphore()
    for device in next_y + next_z + next_x + (across, sibling):
        pl.semaphore_signal(barrier, inc=1, device_id=device, device_id_type=MESH)
    pl.semaphore_wait(barrier, 8)

    def columns(buf, extra=0):
        parts = ((0, 48), (48, 48)), ((96, 48), (144, 48 + extra))
        piece = lambda cut: lambda k1, k2, p: buf.at[k2, k1, pl.ds(*cut[p]), :]
        sizes = [[size // 16 for _, size in cut] for cut in parts]
        return Plane(net, z, next_z, y, next_y, piece(parts[0]), piece(parts[1]), *sizes)

    class Rows:
        def __init__(self, number):
            sent = net.senders()
            piece = lambda k, p: rows.at[number, pl.ds(96 * p, 96), pl.ds((2 * k + core) * TC, TC)]
            self.ring = Ring(net, x, next_x, piece, (6, 6), sent)
            self.pairs, self.end = [], net.group()
            for step in (0, -1, 1, 2):
                k = lax.rem(x + step + 4, 4)
                ref = rows.at[number, :, pl.ds((2 * k + core) * TC, TC)]
                self.pairs.append(net.copy(ref, sibling, sent, 12, self.end))

        def start(self):
            self.ring.start()
            self.pairs[0].start()

        def forward(self):
            self.ring.forward()

        def near(self):
            self.ring.near()
            self.pairs[1].start()
            self.pairs[2].start()

        def far(self):
            self.ring.far()
            self.pairs[3].start()

        def done(self):
            net.wait(self.end)

    spread_rows = (iota((TR, RB), 0) // BLK == iota((TR, RB), 1)).astype(BF)
    spread_cols = (iota((CB, TC), 0) == iota((CB, TC), 1) // BLK).astype(BF)

    def expand(mask):
        wide = mm(mask.astype(F32).astype(BF), spread_cols).astype(BF)
        return mm(spread_rows, wide)

    def own(number):
        return rows.at[number, :, pl.ds(pl.multiple_of(c * TC, TC), TC)]

    def product(number, buf, sign=0):
        if not sign:
            acc[...] = jnp.zeros_like(acc)

        @pl.loop(0, 4)
        def _(k):
            left = rows[number, :, pl.ds(pl.multiple_of(k * 768, 768), 768)]
            right = buf[k, :, pl.ds(0, TR), :].reshape(768, TC)
            if sign:
                acc[...] -= mm(left, right)
            else:
                acc[...] += mm(left, right)

    colp[y, z] = (density[...].astype(F32) * expand(fills[1])).astype(BF)
    get_p = columns(colp)
    get_p.s1()
    row_f, row_s, row_g, row_h = [Rows(number) for number in range(4)]
    masked = (fock[...].astype(F32) * expand(fills[0])).astype(BF)
    own(0)[...] = masked
    row_f.start()
    colf[y, z, pl.ds(0, TR), :] = masked
    masked = (margin[...].astype(F32) * expand(fills[2])).astype(BF)
    own(1)[...] = masked
    row_s.start()
    cols_[y, z] = masked
    get_s, get_f = columns(cols_), columns(colf, 16)
    get_p.s2()
    row_f.forward()
    packed = jnp.zeros((16, TC), F32)
    pad16 = (iota((16, RB), 0) == iota((16, RB), 1)).astype(BF)
    for number in range(TERMS - 1):
        shift = (iota((CB, TC), 1) == CB * number + iota((CB, TC), 0)).astype(BF)
        packed += mm(mm(pad16, seconds[number].astype(F32).astype(BF)).astype(BF), shift)
    colf[y, z, pl.ds(TR, 16), :] = packed.astype(BF)
    get_p.s3()
    row_f.near()
    row_s.forward()
    for number in range(3):
        masks[number] = expand(firsts[number]).astype(BF)
    get_p.s4()
    get_s.s1()
    row_f.far()
    row_s.near()
    row_s.far()
    row_f.done()
    get_p.done()
    get_s.s2()
    product(0, colp)
    own(2)[...] = (acc[...] * masks[0].astype(F32)).astype(BF)
    row_g.start()
    row_s.done()
    get_s.s3()
    product(1, colp)
    own(3)[...] = (acc[...] * masks[1].astype(F32)).astype(BF)
    row_h.start()
    get_s.s4()
    get_f.s1()
    row_g.forward()
    row_g.near()
    row_h.forward()
    row_g.far()
    row_h.near()
    row_h.far()
    row_g.done()
    row_h.done()

    column_block = 24 * y + iota((1, 768), 1) // BLK
    place[...] = jnp.zeros_like(place)

    @pl.loop(0, 16)
    def _(k):
        for i in range(RB):
            place[pl.ds(16 * k + i, 1), :] = (column_block == order[RB * k + i]).astype(F32)

    base = CB * c + 3 * z
    same = lax.rem(iota((BLK, 768), 0), BLK) == lax.rem(iota((BLK, 768), 1), BLK)
    for i in range(3):
        mine = order[base + i]
        for k in range(4):
            hit = jnp.logical_and(same, iota((BLK, 768), 1) // BLK + 24 * k == mine)
            series[0, k, pl.ds(BLK * i, BLK), :] = hit.astype(F32).astype(BF)
        hit = jnp.logical_and(same, iota((BLK, 768), 1) // BLK + 24 * y == mine)
        filters[5, pl.ds(BLK * i, BLK), :] = hit.astype(F32).astype(BF)
    masks[3] = expand(seconds[TERMS - 1]).astype(BF)
    masks[4] = expand(seconds[TERMS]).astype(BF)
    get_s.done()
    get_f.s2()
    product(2, cols_)
    get_f.s3()
    get_f.s4()
    get_f.done()
    product(3, colf, -1)

    tile = (acc[...] * masks[2].astype(F32)).astype(BF)
    panel[x, core, z] = (tile.astype(F32) * 0.25).astype(BF)
    cut = lambda base: lambda k1, k2, p: panel.at[k2, core, k1, pl.ds(base + 48 * p, 48), :]
    get_x = Plane(net, z, next_z, x, next_x, cut(0), cut(96), (3, 3), (3, 3))
    get_x.s1()
    sent, pairs, end = net.senders(), [], net.group()
    for s in (0, -1, 1, 2):
        ref = panel.at[:, core, lax.rem(z + s + 4, 4), pl.ds(0, 96), :]
        pairs.append(net.copy(ref, sibling, sent, 24, end))
    for s in (0, -1, 1, 2):
        ref = panel.at[lax.rem(x + s + 4, 4), core, :, pl.ds(96, 96), :]
        pairs.append(net.copy(ref, sibling, sent, 24, end))
    get_x.s2()
    get_x.s3()
    get_x.s4()
    spread = (iota((16 * 24, 96), 0) - 3 * z).astype(jnp.int32)
    known = colf[:, :, pl.ds(TR, 16), :].reshape(256, TC)
    for number in range(TERMS - 1):
        pick = (spread == CB * number + iota((16 * 24, 96), 1) // BLK).astype(BF)
        wide = mm(known, pick).astype(BF)
        filters[number] = lax.dot_general(
            wide, place[...].astype(BF), (((0,), (0,)), ((), ())), preferred_element_type=F32
        ).astype(BF)
    for number in (0, 4, 1, 2, 5, 6, 3, 7):
        get_x.end(number)
        pairs[number].start()
    net.wait(end)

    def piece_times(step, k, half):
        left = series[step, k, pl.ds(48 * half, 48), :]
        total = None
        for h in range(2):
            part = lax.dot_general(
                left[:, TC * h : TC * (h + 1)], panel[k, h].reshape(768, TC),
                (((1,), (1,)), ((), ())), preferred_element_type=F32,
            )
            total = part if total is None else total + part
        return total

    def filtered(step, half, total):
        cut = pl.ds(48 * half, 48)
        eye = filters[5, cut, :].astype(F32)
        if step == 0:
            return eye + total / float(TERMS)
        return eye + total * filters[step - 1, cut, :].astype(F32) / float(TERMS - step)

    class Turn:
        def __init__(self, step, half):
            self.step, self.half = step, half
            self.near, self.far = net.group(), net.group()
            piece = lambda k, p: series.at[step, k, pl.ds(48 * half, 48), pl.ds(TC * p, TC)]
            self.ring = Ring(net, y, next_y, piece, (3, 3), net.senders(), self.near, self.far)

        def start(self):
            self.ring.start()
            sums[self.half] = piece_times(self.step, y, self.half)

        def forward(self):
            self.ring.forward()

        def finish(self):
            net.wait(self.near)
            total = sums[self.half]
            for s in (-1, 1):
                total += piece_times(self.step, lax.rem(y + s + 4, 4), self.half)
            net.wait(self.far)
            total += piece_times(self.step, lax.rem(y + 2, 4), self.half)
            return filtered(self.step, self.half, total)

    sums = {}

    def put(step, half, value):
        series[step, y, pl.ds(48 * half, 48), :] = value.astype(BF)

    turns = [[Turn(step, half) for half in range(2)] for step in range(1, TERMS)]
    for half in range(2):
        total = piece_times(0, 0, half)
        for k in range(1, 4):
            total += piece_times(0, k, half)
        put(1, half, filtered(0, half, total))
        turns[0][half].start()
    last = []
    for step in range(1, TERMS):
        for half in range(2):
            turns[step - 1][half].forward()
        for half in range(2):
            value = turns[step - 1][half].finish()
            if step < TERMS - 1:
                put(step + 1, half, value)
                turns[step][half].start()
            else:
                last.append(value)

    flat = jnp.concatenate(last, axis=0).T.astype(BF)
    for k in range(4):
        turned[k] = flat[TR * k : TR * (k + 1), :]
    made = []
    for s, device in ((1, next_z[0]), (-1, next_z[1]), (2, across)):
        made.append(net.copy(turned.at[lax.rem(z + s + 4, 4)], device, [net.sem(), 0], 0, None, arrived.at[z]))
    for copy in made:
        copy.start()
    arrived[z] = turned[z]
    for copy in made:
        copy.wait()
    value = jnp.zeros((TR, TC), F32)
    for k in range(4):
        lane = (iota((96, TC), 0) + 96 * k == iota((96, TC), 1)).astype(BF)
        value += mm(arrived[k], lane)
    colt[y, z] = value.astype(BF)
    get_t = columns(colt)
    get_t.s1()
    get_t.s2()
    get_t.s3()
    get_t.s4()
    get_t.done()

    @pl.loop(0, 4)
    def _(k):
        units[pl.ds(48 * k, 48)] = colt[k].reshape(48, 16, TC)

    for b in range(RB):
        for h in range(2):
            own(4)[pl.ds(BLK * b + 16 * h, 16), :] = units[2 * order[r * RB + b] + h]
    row_t = Rows(4)
    row_t.start()
    row_t.forward()
    row_t.near()
    row_t.far()
    row_t.done()
    acc[...] = jnp.zeros_like(acc)

    @pl.loop(0, 4)
    def _(k):
        left = rows[4, :, pl.ds(pl.multiple_of(k * 768, 768), 768)]
        right = jnp.concatenate([units[2 * order[24 * k + b] + h] for b in range(24) for h in range(2)], axis=0)
        acc[...] += mm(left, right)

    value = (acc[...] * masks[3].astype(F32)).astype(BF)
    own(5)[...] = value
    colz[y, z] = value
    row_z, get_z = Rows(5), columns(colz)
    get_z.s1()
    row_z.start()
    get_z.s2()
    row_z.forward()
    get_z.s3()
    row_z.near()
    get_z.s4()
    row_z.far()
    row_z.done()
    get_z.done()
    product(5, colz)
    out[...] = (acc[...] * masks[4].astype(F32)).astype(BF)
    net.finish()
    assert net.used <= SEMS, net.used


def on_device(fock, density, margin, fills, firsts, owner_order, seconds):
    vmem = pl.BlockSpec(memory_space=pltpu.VMEM)
    panel = pltpu.VMEM((4, 4, TR, TC), BF)
    return pl.pallas_call(
        body,
        out_shape=jax.ShapeDtypeStruct((TR, TC), BF),
        in_specs=[vmem] * 6 + [pl.BlockSpec(memory_space=pltpu.SMEM)],
        out_specs=vmem,
        scratch_shapes=[
            panel,
            panel,
            pltpu.VMEM((4, 4, TR + 16, TC), BF),
            panel,
            panel,
            pltpu.VMEM((4, 2, 4, TR, TC), BF),
            pltpu.VMEM((TERMS, 4, 96, 768), BF),
            pltpu.VMEM((192, 16, TC), BF),
            pltpu.VMEM((6, TR, N), BF),
            pltpu.VMEM((TR, TC), F32),
            pltpu.VMEM((5, TR, TC), BF),
            pltpu.VMEM((6, 96, 768), BF),
            pltpu.VMEM((256, 768), F32),
            pltpu.VMEM((4, TR, 96), BF),
            pltpu.VMEM((4, TR, 96), BF),
            pltpu.SemaphoreType.DMA((SEMS,)),
        ],
        compiler_params=pltpu.CompilerParams(
            collective_id=0, has_side_effects=True, vmem_limit_bytes=60 * 1024 * 1024
        ),
    )(fock, density, margin, fills, firsts, seconds, owner_order)


def solution(mesh):
    return jax.shard_map(
        on_device,
        mesh=mesh,
        in_specs=(
            P("row", "col"),
            P("row", "col"),
            P("row", "col"),
            P(None, "row", "col"),
            P(None, "row", "col"),
            P(),
            P(None, "row", "col"),
        ),
        out_specs=P("row", "col"),
        check_vma=False,
    )
```

```python
import jax
import jax.numpy as jnp
from jax import lax
from jax.experimental import pallas as pl
from jax.experimental.pallas import tpu as pltpu
from jax.sharding import PartitionSpec as P

MESH = pl.DeviceIdType.MESH
BLK = 32
TERMS = 6
RB = 6
CB = 12
TR = 192
TC = 384
N = 3072
NB = 96
SEMS = 154
BF = jnp.bfloat16
F32 = jnp.float32


def iota(shape, axis):
    return lax.broadcasted_iota(jnp.int32, shape, axis)


def mm(a, b):
    return jnp.dot(a, b, preferred_element_type=F32)


class Net:
    def __init__(self, sems, units):
        self.sems, self.units, self.used, self.groups = sems, units, 0, []
        self.spare, self.taken = [], []

    def sem(self):
        if self.spare:
            made = self.spare.pop(0)
        else:
            made = self.used
            self.used += 1
        self.taken.append(made)
        return self.sems.at[made]

    def release(self, owner):
        for sent in owner.sends:
            self.wait(sent)
            self.groups = [made for made in self.groups if made is not sent]
        self.spare.extend(owner.held)

    def group(self):
        made = [self.sem(), 0]
        return made

    def senders(self):
        made = self.group()
        self.groups.append(made)
        return made

    def copy(self, ref, device, sent, size, got=None, target=None):
        if got is None:
            got = self.sem()
        elif isinstance(got, list):
            got[1] += size
            got = got[0]
        sent[1] += size
        return pltpu.make_async_remote_copy(
            ref, ref if target is None else target, sent[0], got, device_id=device, device_id_type=MESH
        )

    def wait(self, group):
        ref = self.units.at[pl.ds(0, group[1])]
        pltpu.make_async_copy(ref, ref, group[0]).wait()

    def finish(self):
        for made in self.groups:
            self.wait(made)


class Ring:
    def __init__(self, net, k, nexts, piece, sizes, sent, near=None, far=None):
        after, before = nexts
        p = lambda step, part: piece(lax.rem(k + step + 4, 4), part)
        c = lambda step, part, device, got=None: net.copy(p(step, part), device, sent, sizes[part], got)
        self.a0, self.b1 = c(0, 0, after), c(0, 1, before)
        self.a1, self.b0 = c(0, 1, after, near), c(0, 0, before, near)
        self.f0, self.f1 = c(-1, 0, after, far), c(1, 1, before, far)

    def start(self):
        for made in (self.a0, self.b1, self.a1, self.b0):
            made.start()

    def forward(self):
        self.a0.wait_recv()
        self.f0.start()
        self.b1.wait_recv()
        self.f1.start()

    def near(self):
        self.a1.wait_recv()
        self.b0.wait_recv()

    def far(self):
        self.f0.wait_recv()
        self.f1.wait_recv()


class Plane:
    def __init__(self, net, k1, next1, k2, next2, piece_a, piece_b, sizes_a, sizes_b):
        self.net = net
        net.taken = []
        sends = [net.senders(), net.senders()]
        turn = lambda k, s: lax.rem(k + s + 4, 4)
        steps = (0, -1, 1, 2)
        self.ends = []

        def second(k, nexts, piece, sizes, sent):
            rings = []
            for s in steps:
                end = net.group()
                self.ends.append(end)
                rings.append(Ring(net, k, nexts, piece(s), sizes, sent, end, end))
            return rings

        self.a1 = Ring(net, k1, next1, lambda k, p: piece_a(k, k2, p), sizes_a, sends[0])
        self.a2 = second(k2, next2, lambda s: lambda k, p: piece_a(turn(k1, s), k, p), sizes_a, sends[0])
        self.b1 = Ring(net, k2, next2, lambda k, p: piece_b(k1, k, p), sizes_b, sends[1])
        self.b2 = second(k1, next1, lambda s: lambda k, p: piece_b(k, turn(k2, s), p), sizes_b, sends[1])
        self.sends, self.held = sends, net.taken

    def s1(self):
        self.a1.start()
        self.b1.start()
        self.a2[0].start()
        self.b2[0].start()

    def s2(self):
        self.a1.forward()
        self.b1.forward()
        for first, rings in ((self.a1, self.a2), (self.b1, self.b2)):
            first.near()
            rings[1].start()
            rings[2].start()

    def s3(self):
        self.a2[0].forward()
        self.b2[0].forward()
        for first, rings in ((self.a1, self.a2), (self.b1, self.b2)):
            first.far()
            rings[3].start()

    def s4(self):
        for number in (1, 2, 3):
            self.a2[number].forward()
            self.b2[number].forward()

    def end(self, number):
        self.net.wait(self.ends[number])

    def done(self):
        for number in range(8):
            self.end(number)


def body(
    fock, density, margin, fills, firsts, seconds, order, out,
    colp, cols_, colf, colt, colz, panel, series, units, rows, acc, masks, filters, place, turned, arrived, sems,
):
    r, c = lax.axis_index("row"), lax.axis_index("col")
    y, z = r // 4, lax.rem(r, 4)
    x, core = c // 2, lax.rem(c, 2)
    net = Net(sems, units)

    def dev(yy, zz, xx):
        return (lax.rem(yy + 4, 4) * 4 + lax.rem(zz + 4, 4), lax.rem(xx + 4, 4) * 2 + core)

    next_y = (dev(y + 1, z, x), dev(y - 1, z, x))
    next_z = (dev(y, z + 1, x), dev(y, z - 1, x))
    next_x = (dev(y, z, x + 1), dev(y, z, x - 1))
    across = dev(y, z + 2, x)
    sibling = (r, 2 * x + 1 - core)

    barrier = pltpu.get_barrier_semaphore()
    for device in next_y + next_z + next_x + (across, sibling):
        pl.semaphore_signal(barrier, inc=1, device_id=device, device_id_type=MESH)
    pl.semaphore_wait(barrier, 8)

    def columns(buf, extra=0):
        parts = ((0, 48), (48, 48)), ((96, 48), (144, 48 + extra))
        piece = lambda cut: lambda k1, k2, p: buf.at[k2, k1, pl.ds(*cut[p]), :]
        sizes = [[size // 16 for _, size in cut] for cut in parts]
        return Plane(net, z, next_z, y, next_y, piece(parts[0]), piece(parts[1]), *sizes)

    class Rows:
        def __init__(self, number):
            net.taken = []
            sent = net.senders()
            piece = lambda k, p: rows.at[number, pl.ds(96 * p, 96), pl.ds((2 * k + core) * TC, TC)]
            self.ring = Ring(net, x, next_x, piece, (6, 6), sent)
            self.ends = [net.group(), net.group(), net.group()]
            turn = lambda s: lax.rem(x + s + 4, 4)
            give = lambda s, p, end: net.copy(piece(turn(s), p), sibling, sent, 6, self.ends[end])
            self.own = (give(0, 0, 0), give(0, 1, 0))
            self.nears = (give(-1, 0, 1), give(1, 1, 1), give(-1, 1, 1), give(1, 0, 1))
            self.fars = (give(2, 0, 2), give(2, 1, 2))
            self.sends, self.held = [sent], net.taken

        def start(self):
            self.ring.start()
            for made in self.own:
                made.start()

        def forward(self):
            ring = self.ring
            for got, further, give in ((ring.a0, ring.f0, 0), (ring.b1, ring.f1, 1)):
                got.wait_recv()
                further.start()
                self.nears[give].start()

        def near(self):
            for got, give in ((self.ring.a1, 2), (self.ring.b0, 3)):
                got.wait_recv()
                self.nears[give].start()

        def far(self):
            for got, give in ((self.ring.f0, 0), (self.ring.f1, 1)):
                got.wait_recv()
                self.fars[give].start()

        def done(self):
            for end in self.ends:
                net.wait(end)

    spread_rows = (iota((TR, RB), 0) // BLK == iota((TR, RB), 1)).astype(BF)
    spread_cols = (iota((CB, TC), 0) == iota((CB, TC), 1) // BLK).astype(BF)

    def expand(mask):
        wide = mm(mask.astype(F32).astype(BF), spread_cols).astype(BF)
        return mm(spread_rows, wide)

    def own(number):
        return rows.at[number, :, pl.ds(pl.multiple_of(c * TC, TC), TC)]

    def product(number, buf, sign=0):
        if not sign:
            acc[...] = jnp.zeros_like(acc)

        @pl.loop(0, 4)
        def _(k):
            left = rows[number, :, pl.ds(pl.multiple_of(k * 768, 768), 768)]
            right = buf[k, :, pl.ds(0, TR), :].reshape(768, TC)
            if sign:
                acc[...] -= mm(left, right)
            else:
                acc[...] += mm(left, right)

    colp[y, z] = (density[...].astype(F32) * expand(fills[1])).astype(BF)
    get_p = columns(colp)
    get_p.s1()
    row_f, row_s, row_g, row_h = [Rows(number) for number in range(4)]
    masked = (fock[...].astype(F32) * expand(fills[0])).astype(BF)
    own(0)[...] = masked
    row_f.start()
    colf[y, z] = masked
    masked = (margin[...].astype(F32) * expand(fills[2])).astype(BF)
    own(1)[...] = masked
    row_s.start()
    cols_[y, z, pl.ds(0, TR), :] = masked
    get_s, get_f = columns(cols_, 16), columns(colf)
    get_p.s2()
    row_f.forward()
    packed = jnp.zeros((16, TC), F32)
    pad16 = (iota((16, RB), 0) == iota((16, RB), 1)).astype(BF)
    for number in range(TERMS - 1):
        shift = (iota((CB, TC), 1) == CB * number + iota((CB, TC), 0)).astype(BF)
        packed += mm(mm(pad16, seconds[:, number, :].astype(F32).astype(BF)).astype(BF), shift)
    cols_[y, z, pl.ds(TR, 16), :] = packed.astype(BF)
    get_p.s3()
    row_f.near()
    row_s.forward()
    for number in range(3):
        masks[number] = expand(firsts[number]).astype(BF)
    get_p.s4()
    get_s.s1()
    row_f.far()
    row_s.near()
    row_s.far()
    row_f.done()
    get_p.done()
    get_s.s2()
    product(0, colp)
    own(2)[...] = (acc[...] * masks[0].astype(F32)).astype(BF)
    row_g.start()
    row_s.done()
    get_s.s3()
    product(1, colp)
    own(3)[...] = (acc[...] * masks[1].astype(F32)).astype(BF)
    row_h.start()
    get_s.s4()
    get_f.s1()
    row_g.forward()
    row_g.near()
    row_h.forward()
    net.release(get_p)
    net.release(row_f)
    net.release(row_s)
    column_block = 24 * y + iota((1, 768), 1) // BLK
    place[...] = jnp.zeros_like(place)

    @pl.loop(0, 16)
    def _(k):
        for i in range(RB):
            place[pl.ds(16 * k + i, 1), :] = (column_block == order[RB * k + i]).astype(F32)

    base = CB * c + 3 * z
    same = lax.rem(iota((BLK, 768), 0), BLK) == lax.rem(iota((BLK, 768), 1), BLK)
    for i in range(3):
        mine = order[base + i]
        for k in range(4):
            hit = jnp.logical_and(same, iota((BLK, 768), 1) // BLK + 24 * k == mine)
            series[0, k, pl.ds(BLK * i, BLK), :] = hit.astype(F32).astype(BF)
        hit = jnp.logical_and(same, iota((BLK, 768), 1) // BLK + 24 * y == mine)
        filters[5, pl.ds(BLK * i, BLK), :] = hit.astype(F32).astype(BF)
    masks[3] = expand(seconds[:, TERMS - 1, :]).astype(BF)
    masks[4] = expand(seconds[:, TERMS, :]).astype(BF)
    get_s.done()
    get_f.s2()
    row_g.far()
    row_h.near()
    get_f.s3()
    row_h.far()
    row_g.done()
    get_f.s4()
    known = cols_[:, :, pl.ds(TR, 16), :].reshape(256, TC)
    spread = iota((TC, 96), 0) - 3 * z
    for number in range(TERMS - 1):
        pick = (spread == CB * number + iota((TC, 96), 1) // BLK).astype(BF)
        wide = mm(known, pick).astype(BF)
        filters[number] = lax.dot_general(
            wide, place[...].astype(BF), (((0,), (0,)), ((), ())), preferred_element_type=F32
        ).astype(BF)
    product(2, cols_)
    row_h.done()
    get_f.done()
    product(3, colf, -1)

    tile = (acc[...] * masks[2].astype(F32)).astype(BF)
    panel[x, core, z] = (tile.astype(F32) * 0.25).astype(BF)
    cut = lambda base: lambda k1, k2, p: panel.at[k2, core, k1, pl.ds(base + 48 * p, 48), :]
    get_x = Plane(net, z, next_z, x, next_x, cut(0), cut(96), (3, 3), (3, 3))
    get_x.s1()
    sent, pairs, end = net.senders(), [], net.group()
    for s in (0, -1, 1, 2):
        ref = panel.at[:, core, lax.rem(z + s + 4, 4), pl.ds(0, 96), :]
        pairs.append(net.copy(ref, sibling, sent, 24, end))
    for s in (0, -1, 1, 2):
        ref = panel.at[lax.rem(x + s + 4, 4), core, :, pl.ds(96, 96), :]
        pairs.append(net.copy(ref, sibling, sent, 24, end))
    get_x.s2()
    get_x.s3()
    get_x.s4()
    for number in (0, 4, 1, 2, 5, 6, 3, 7):
        get_x.end(number)
        pairs[number].start()
    net.release(get_s)
    net.release(get_f)
    net.release(row_g)
    net.release(row_h)
    net.wait(end)
    net.release(get_x)

    def piece_times(step, k, half):
        left = series[step, k] if half is None else series[step, k, pl.ds(48 * half, 48), :]
        total = None
        for h in range(2):
            part = lax.dot_general(
                left[:, TC * h : TC * (h + 1)], panel[k, h].reshape(768, TC),
                (((1,), (1,)), ((), ())), preferred_element_type=F32,
            )
            total = part if total is None else total + part
        return total

    def filtered(step, half, total):
        cut = pl.ds(0, 96) if half is None else pl.ds(48 * half, 48)
        eye = filters[5, cut, :].astype(F32)
        if step == 0:
            return eye + total / float(TERMS)
        return eye + total * filters[step - 1, cut, :].astype(F32) / float(TERMS - step)

    class Turn:
        def __init__(self, step, half):
            self.step, self.half = step, half
            self.near, self.far = net.group(), net.group()
            piece = lambda k, p: series.at[step, k, pl.ds(48 * half, 48), pl.ds(TC * p, TC)]
            self.ring = Ring(net, y, next_y, piece, (3, 3), net.senders(), self.near, self.far)

        def start(self):
            self.ring.start()
            sums[self.half] = piece_times(self.step, y, self.half)

        def forward(self):
            self.ring.forward()

        def finish(self):
            net.wait(self.near)
            total = sums[self.half]
            for s in (-1, 1):
                total += piece_times(self.step, lax.rem(y + s + 4, 4), self.half)
            net.wait(self.far)
            total += piece_times(self.step, lax.rem(y + 2, 4), self.half)
            return filtered(self.step, self.half, total)

    sums = {}

    def put(step, half, value):
        series[step, y, pl.ds(48 * half, 48), :] = value.astype(BF)

    turns = [[Turn(step, half) for half in range(2)] for step in range(1, TERMS)]
    total = piece_times(0, 0, None)
    for k in range(1, 4):
        total += piece_times(0, k, None)
    series[1, y] = filtered(0, None, total).astype(BF)
    last = [None, None]

    def finish(step, half):
        value = turns[step - 1][half].finish()
        if step < TERMS - 1:
            put(step + 1, half, value)
            turns[step][half].start()
        else:
            last[half] = value

    turns[0][0].start()
    turns[0][0].forward()
    turns[0][1].start()
    for step in range(1, TERMS):
        finish(step, 0)
        turns[step - 1][1].forward()
        if step < TERMS - 1:
            turns[step][0].forward()
        finish(step, 1)

    flat = jnp.concatenate(last, axis=0).T.astype(BF)
    for k in range(4):
        turned[k] = flat[TR * k : TR * (k + 1), :]
    made = []
    for s, device in ((1, next_z[0]), (-1, next_z[1]), (2, across)):
        made.append(net.copy(turned.at[lax.rem(z + s + 4, 4)], device, [net.sem(), 0], 0, None, arrived.at[z]))
    for copy in made:
        copy.start()
    arrived[z] = turned[z]
    for copy in made:
        copy.wait()
    value = jnp.zeros((TR, TC), F32)
    for k in range(4):
        lane = (iota((96, TC), 0) + 96 * k == iota((96, TC), 1)).astype(BF)
        value += mm(arrived[k], lane)
    colt[y, z] = value.astype(BF)
    get_t = columns(colt)
    get_t.s1()
    get_t.s2()
    get_t.s3()
    get_t.s4()
    get_t.done()

    @pl.loop(0, 4)
    def _(k):
        units[pl.ds(48 * k, 48)] = colt[k].reshape(48, 16, TC)

    for b in range(RB):
        for h in range(2):
            own(4)[pl.ds(BLK * b + 16 * h, 16), :] = units[2 * order[r * RB + b] + h]
    row_t = Rows(4)
    row_t.start()
    row_t.forward()
    acc[...] = jnp.zeros_like(acc)

    def accumulate(k):
        left = rows[4, :, pl.ds(pl.multiple_of(k * 768, 768), 768)]
        right = jnp.concatenate([units[2 * order[24 * k + b] + h] for b in range(24) for h in range(2)], axis=0)
        acc[...] += mm(left, right)

    net.wait(row_t.ends[0])
    accumulate(x)
    row_t.near()
    net.wait(row_t.ends[1])
    accumulate(lax.rem(x + 1, 4))
    row_t.far()
    accumulate(lax.rem(x + 3, 4))
    net.wait(row_t.ends[2])
    accumulate(lax.rem(x + 2, 4))
    value = (acc[...] * masks[3].astype(F32)).astype(BF)
    own(5)[...] = value
    colz[y, z] = value
    row_z, get_z = Rows(5), columns(colz)
    get_z.s1()
    row_z.start()
    get_z.s2()
    row_z.forward()
    get_z.s3()
    row_z.near()
    get_z.s4()
    row_z.far()
    row_z.done()
    get_z.done()
    product(5, colz)
    out[...] = (acc[...] * masks[4].astype(F32)).astype(BF)
    net.finish()
    assert net.used <= SEMS, net.used


def on_device(fock, density, margin, fills, firsts, owner_order, seconds):
    vmem = pl.BlockSpec(memory_space=pltpu.VMEM)
    panel = pltpu.VMEM((4, 4, TR, TC), BF)
    return pl.pallas_call(
        body,
        out_shape=jax.ShapeDtypeStruct((TR, TC), BF),
        in_specs=[vmem] * 6 + [pl.BlockSpec(memory_space=pltpu.SMEM)],
        out_specs=vmem,
        scratch_shapes=[
            panel,
            pltpu.VMEM((4, 4, TR + 16, TC), BF),
            panel,
            panel,
            panel,
            pltpu.VMEM((4, 2, 4, TR, TC), BF),
            pltpu.VMEM((TERMS, 4, 96, 768), BF),
            pltpu.VMEM((192, 16, TC), BF),
            pltpu.VMEM((6, TR, N), BF),
            pltpu.VMEM((TR, TC), F32),
            pltpu.VMEM((5, TR, TC), BF),
            pltpu.VMEM((6, 96, 768), BF),
            pltpu.VMEM((256, 768), F32),
            pltpu.VMEM((4, TR, 96), BF),
            pltpu.VMEM((4, TR, 96), BF),
            pltpu.SemaphoreType.DMA((SEMS,)),
        ],
        compiler_params=pltpu.CompilerParams(
            collective_id=0, has_side_effects=True, vmem_limit_bytes=60 * 1024 * 1024
        ),
    )(fock, density, margin, fills, firsts, jnp.swapaxes(seconds, 0, 1), owner_order)


def solution(mesh):
    return jax.shard_map(
        on_device,
        mesh=mesh,
        in_specs=(
            P("row", "col"),
            P("row", "col"),
            P("row", "col"),
            P(None, "row", "col"),
            P(None, "row", "col"),
            P(),
            P(None, "row", "col"),
        ),
        out_specs=P("row", "col"),
        check_vma=False,
    )
```

```python
import jax
import jax.numpy as jnp
from jax import lax
from jax.experimental import pallas as pl
from jax.experimental.pallas import tpu as pltpu
from jax.sharding import PartitionSpec as P

MESH = pl.DeviceIdType.MESH
BLK = 32
TERMS = 6
RB = 6
CB = 12
TR = 192
TC = 384
N = 3072
NB = 96
SEMS = 154
BF = jnp.bfloat16
F32 = jnp.float32


def iota(shape, axis):
    return lax.broadcasted_iota(jnp.int32, shape, axis)


def mm(a, b):
    return jnp.dot(a, b, preferred_element_type=F32)


class Net:
    def __init__(self, sems, units):
        self.sems, self.units, self.used, self.groups = sems, units, 0, []
        self.spare, self.taken = [], []

    def sem(self):
        if self.spare:
            made = self.spare.pop(0)
        else:
            made = self.used
            self.used += 1
        self.taken.append(made)
        return self.sems.at[made]

    def release(self, owner):
        for sent in owner.sends:
            self.wait(sent)
            self.groups = [made for made in self.groups if made is not sent]
        self.spare.extend(owner.held)

    def group(self):
        made = [self.sem(), 0]
        return made

    def senders(self):
        made = self.group()
        self.groups.append(made)
        return made

    def copy(self, ref, device, sent, size, got=None, target=None):
        if got is None:
            got = self.sem()
        elif isinstance(got, list):
            got[1] += size
            got = got[0]
        sent[1] += size
        return pltpu.make_async_remote_copy(
            ref, ref if target is None else target, sent[0], got, device_id=device, device_id_type=MESH
        )

    def wait(self, group):
        ref = self.units.at[pl.ds(0, group[1])]
        pltpu.make_async_copy(ref, ref, group[0]).wait()

    def finish(self):
        for made in self.groups:
            self.wait(made)


class Ring:
    def __init__(self, net, k, nexts, piece, sizes, sent, near=None, far=None):
        after, before = nexts
        p = lambda step, part: piece(lax.rem(k + step + 4, 4), part)
        c = lambda step, part, device, got=None: net.copy(p(step, part), device, sent, sizes[part], got)
        self.a0, self.b1 = c(0, 0, after), c(0, 1, before)
        self.a1, self.b0 = c(0, 1, after, near), c(0, 0, before, near)
        self.f0, self.f1 = c(-1, 0, after, far), c(1, 1, before, far)

    def start(self):
        for made in (self.a0, self.b1, self.a1, self.b0):
            made.start()

    def forward(self):
        self.a0.wait_recv()
        self.f0.start()
        self.b1.wait_recv()
        self.f1.start()

    def near(self):
        self.a1.wait_recv()
        self.b0.wait_recv()

    def far(self):
        self.f0.wait_recv()
        self.f1.wait_recv()


class Plane:
    def __init__(self, net, k1, next1, k2, next2, piece_a, piece_b, sizes_a, sizes_b):
        self.net = net
        net.taken = []
        sends = [net.senders(), net.senders()]
        turn = lambda k, s: lax.rem(k + s + 4, 4)
        steps = (0, -1, 1, 2)
        self.ends = []

        def second(k, nexts, piece, sizes, sent):
            rings = []
            for s in steps:
                end = net.group()
                self.ends.append(end)
                rings.append(Ring(net, k, nexts, piece(s), sizes, sent, end, end))
            return rings

        self.a1 = Ring(net, k1, next1, lambda k, p: piece_a(k, k2, p), sizes_a, sends[0])
        self.a2 = second(k2, next2, lambda s: lambda k, p: piece_a(turn(k1, s), k, p), sizes_a, sends[0])
        self.b1 = Ring(net, k2, next2, lambda k, p: piece_b(k1, k, p), sizes_b, sends[1])
        self.b2 = second(k1, next1, lambda s: lambda k, p: piece_b(k, turn(k2, s), p), sizes_b, sends[1])
        self.sends, self.held = sends, net.taken

    def s1(self):
        self.a1.start()
        self.b1.start()
        self.a2[0].start()
        self.b2[0].start()

    def s2(self):
        self.a1.forward()
        self.b1.forward()
        for first, rings in ((self.a1, self.a2), (self.b1, self.b2)):
            first.near()
            rings[1].start()
            rings[2].start()

    def s3(self):
        self.a2[0].forward()
        self.b2[0].forward()
        for first, rings in ((self.a1, self.a2), (self.b1, self.b2)):
            first.far()
            rings[3].start()

    def s4(self):
        for number in (1, 2, 3):
            self.a2[number].forward()
            self.b2[number].forward()

    def end(self, number):
        self.net.wait(self.ends[number])

    def done(self):
        for number in range(8):
            self.end(number)


def body(
    fock, density, margin, fills, firsts, seconds, order, out,
    colp, cols_, colf, colt, colz, panel, series, units, rows, acc, masks, filters, place, sems,
):
    r, c = lax.axis_index("row"), lax.axis_index("col")
    y, z = r // 4, lax.rem(r, 4)
    x, core = c // 2, lax.rem(c, 2)
    net = Net(sems, units)

    def dev(yy, zz, xx):
        return (lax.rem(yy + 4, 4) * 4 + lax.rem(zz + 4, 4), lax.rem(xx + 4, 4) * 2 + core)

    next_y = (dev(y + 1, z, x), dev(y - 1, z, x))
    next_z = (dev(y, z + 1, x), dev(y, z - 1, x))
    next_x = (dev(y, z, x + 1), dev(y, z, x - 1))
    sibling = (r, 2 * x + 1 - core)

    barrier = pltpu.get_barrier_semaphore()
    for device in next_y + next_z + next_x + (sibling,):
        pl.semaphore_signal(barrier, inc=1, device_id=device, device_id_type=MESH)
    pl.semaphore_wait(barrier, 7)

    def columns(buf, extra=0):
        parts = ((0, 48), (48, 48)), ((96, 48), (144, 48 + extra))
        piece = lambda cut: lambda k1, k2, p: buf.at[k2, k1, pl.ds(*cut[p]), :]
        sizes = [[size // 16 for _, size in cut] for cut in parts]
        return Plane(net, z, next_z, y, next_y, piece(parts[0]), piece(parts[1]), *sizes)

    class Rows:
        def __init__(self, number):
            net.taken = []
            sent = net.senders()
            piece = lambda k, p: rows.at[number, pl.ds(96 * p, 96), pl.ds((2 * k + core) * TC, TC)]
            self.ring = Ring(net, x, next_x, piece, (6, 6), sent)
            self.ends = [net.group(), net.group(), net.group()]
            turn = lambda s: lax.rem(x + s + 4, 4)
            give = lambda s, p, end: net.copy(piece(turn(s), p), sibling, sent, 6, self.ends[end])
            self.own = (give(0, 0, 0), give(0, 1, 0))
            self.nears = (give(-1, 0, 1), give(1, 1, 1), give(-1, 1, 1), give(1, 0, 1))
            self.fars = (give(2, 0, 2), give(2, 1, 2))
            self.sends, self.held = [sent], net.taken

        def start(self):
            self.ring.start()
            for made in self.own:
                made.start()

        def forward(self):
            ring = self.ring
            for got, further, give in ((ring.a0, ring.f0, 0), (ring.b1, ring.f1, 1)):
                got.wait_recv()
                further.start()
                self.nears[give].start()

        def near(self):
            for got, give in ((self.ring.a1, 2), (self.ring.b0, 3)):
                got.wait_recv()
                self.nears[give].start()

        def far(self):
            for got, give in ((self.ring.f0, 0), (self.ring.f1, 1)):
                got.wait_recv()
                self.fars[give].start()

        def done(self):
            for end in self.ends:
                net.wait(end)

    spread_rows = (iota((TR, RB), 0) // BLK == iota((TR, RB), 1)).astype(BF)
    spread_cols = (iota((CB, TC), 0) == iota((CB, TC), 1) // BLK).astype(BF)

    def expand(mask):
        wide = mm(mask.astype(F32).astype(BF), spread_cols).astype(BF)
        return mm(spread_rows, wide)

    def own(number):
        return rows.at[number, :, pl.ds(pl.multiple_of(c * TC, TC), TC)]

    def product(number, buf, sign=0):
        if not sign:
            acc[...] = jnp.zeros_like(acc)

        @pl.loop(0, 4)
        def _(k):
            left = rows[number, :, pl.ds(pl.multiple_of(k * 768, 768), 768)]
            right = buf[k, :, pl.ds(0, TR), :].reshape(768, TC)
            if sign:
                acc[...] -= mm(left, right)
            else:
                acc[...] += mm(left, right)

    colp[y, z] = (density[...].astype(F32) * expand(fills[1])).astype(BF)
    get_p = columns(colp)
    get_p.s1()
    row_f, row_s, row_g, row_h = [Rows(number) for number in range(4)]
    masked = (fock[...].astype(F32) * expand(fills[0])).astype(BF)
    own(0)[...] = masked
    row_f.start()
    colf[y, z] = masked
    masked = (margin[...].astype(F32) * expand(fills[2])).astype(BF)
    own(1)[...] = masked
    row_s.start()
    cols_[y, z, pl.ds(0, TR), :] = masked
    get_s, get_f = columns(cols_, 16), columns(colf)
    get_p.s2()
    row_f.forward()
    packed = jnp.zeros((16, TC), F32)
    pad16 = (iota((16, RB), 0) == iota((16, RB), 1)).astype(BF)
    for number in range(TERMS - 1):
        shift = (iota((CB, TC), 1) == CB * number + iota((CB, TC), 0)).astype(BF)
        packed += mm(mm(pad16, seconds[:, number, :].astype(F32).astype(BF)).astype(BF), shift)
    cols_[y, z, pl.ds(TR, 16), :] = packed.astype(BF)
    get_p.s3()
    row_f.near()
    row_s.forward()
    for number in range(3):
        masks[number] = expand(firsts[number]).astype(BF)
    get_p.s4()
    get_s.s1()
    row_f.far()
    row_s.near()
    row_s.far()
    row_f.done()
    get_p.done()
    get_s.s2()
    product(0, colp)
    own(2)[...] = (acc[...] * masks[0].astype(F32)).astype(BF)
    row_g.start()
    row_s.done()
    get_s.s3()
    product(1, colp)
    own(3)[...] = (acc[...] * masks[1].astype(F32)).astype(BF)
    row_h.start()
    get_s.s4()
    get_f.s1()
    row_g.forward()
    row_g.near()
    row_h.forward()
    net.release(get_p)
    net.release(row_f)
    net.release(row_s)
    column_block = 24 * y + iota((1, 768), 1) // BLK
    place[...] = jnp.zeros_like(place)

    @pl.loop(0, 16)
    def _(k):
        for i in range(RB):
            place[pl.ds(16 * k + i, 1), :] = (column_block == order[RB * k + i]).astype(F32)

    base = CB * c + 3 * z
    same = lax.rem(iota((BLK, 768), 0), BLK) == lax.rem(iota((BLK, 768), 1), BLK)
    for i in range(3):
        mine = order[base + i]
        for k in range(4):
            hit = jnp.logical_and(same, iota((BLK, 768), 1) // BLK + 24 * k == mine)
            series[0, k, pl.ds(BLK * i, BLK), :] = hit.astype(F32).astype(BF)
        hit = jnp.logical_and(same, iota((BLK, 768), 1) // BLK + 24 * y == mine)
        filters[5, pl.ds(BLK * i, BLK), :] = hit.astype(F32).astype(BF)
    masks[3] = expand(seconds[:, TERMS - 1, :]).astype(BF)
    masks[4] = expand(seconds[:, TERMS, :]).astype(BF)
    get_s.done()
    get_f.s2()
    row_g.far()
    row_h.near()
    get_f.s3()
    row_h.far()
    row_g.done()
    get_f.s4()
    known = cols_[:, :, pl.ds(TR, 16), :].reshape(256, TC)
    spread = iota((TC, 96), 0) - 3 * z
    for number in range(TERMS - 1):
        pick = (spread == CB * number + iota((TC, 96), 1) // BLK).astype(BF)
        wide = mm(known, pick).astype(BF)
        filters[number] = lax.dot_general(
            wide, place[...].astype(BF), (((0,), (0,)), ((), ())), preferred_element_type=F32
        ).astype(BF)
    product(2, cols_)
    row_h.done()
    get_f.done()
    product(3, colf, -1)
    net.release(get_s)
    net.release(get_f)
    net.release(row_g)
    net.release(row_h)

    tile = (acc[...] * masks[2].astype(F32)).astype(BF)
    side = pl.ds(pl.multiple_of(core * TC, TC), TC)
    panel[x, z, :, side] = (tile.astype(F32) * 0.25).astype(BF)
    cut = lambda base: lambda k1, k2, p: panel.at[k2, k1, pl.ds(base + 48 * p, 48), side]
    get_x = Plane(net, z, next_z, x, next_x, cut(0), cut(96), (3, 3), (3, 3))
    get_x.s1()
    sent, pairs, end = net.senders(), [], net.group()
    for s in (0, -1, 1, 2):
        ref = panel.at[:, lax.rem(z + s + 4, 4), pl.ds(0, 96), side]
        pairs.append(net.copy(ref, sibling, sent, 24, end))
    for s in (0, -1, 1, 2):
        ref = panel.at[lax.rem(x + s + 4, 4), :, pl.ds(96, 96), side]
        pairs.append(net.copy(ref, sibling, sent, 24, end))
    get_x.s2()
    get_x.s3()
    get_x.s4()
    for number in (0, 4, 1, 2, 5, 6, 3, 7):
        get_x.end(number)
        pairs[number].start()
    net.wait(end)
    net.release(get_x)

    def piece_times(step, k, half):
        left = series[step, k] if half is None else series[step, k, pl.ds(48 * half, 48), :]
        return lax.dot_general(
            left, panel[k].reshape(768, 768), (((1,), (1,)), ((), ())), preferred_element_type=F32
        )

    def filtered(step, half, total):
        cut = pl.ds(0, 96) if half is None else pl.ds(48 * half, 48)
        eye = filters[5, cut, :].astype(F32)
        if step == 0:
            return eye + total / float(TERMS)
        return eye + total * filters[step - 1, cut, :].astype(F32) / float(TERMS - step)

    class Turn:
        def __init__(self, step, half):
            self.step, self.half = step, half
            self.near, self.far = net.group(), net.group()
            piece = lambda k, p: series.at[step, k, pl.ds(48 * half, 48), pl.ds(TC * p, TC)]
            self.ring = Ring(net, y, next_y, piece, (3, 3), net.senders(), self.near, self.far)

        def start(self):
            self.ring.start()
            sums[self.half] = piece_times(self.step, y, self.half)

        def forward(self):
            self.ring.forward()

        def middle(self):
            net.wait(self.near)
            for s in (-1, 1):
                sums[self.half] += piece_times(self.step, lax.rem(y + s + 4, 4), self.half)

        def finish(self):
            net.wait(self.far)
            total = sums[self.half] + piece_times(self.step, lax.rem(y + 2, 4), self.half)
            return filtered(self.step, self.half, total)

    sums = {}

    def put(step, half, value):
        series[step, y, pl.ds(48 * half, 48), :] = value.astype(BF)

    turns = [[Turn(step, half) for half in range(2)] for step in range(1, TERMS)]
    total = piece_times(0, 0, None)
    for k in range(1, 4):
        total += piece_times(0, k, None)
    series[1, y] = filtered(0, None, total).astype(BF)
    cut = lambda base: lambda k1, k2, p: colt.at[k2, k1, pl.ds(base, 48), pl.ds(TC * p, TC)]
    get_t = Plane(net, z, next_z, y, next_y, cut(0), cut(48), (3, 3), (3, 3))

    def finish(step, half):
        value = turns[step - 1][half].finish()
        if step < TERMS - 1:
            put(step + 1, half, value)
            turns[step][half].start()
        else:
            colt[y, z, pl.ds(48 * half, 48), :] = value.astype(BF)
            for ring in ((get_t.a1, get_t.a2[0]), (get_t.b1, get_t.b2[0]))[half]:
                ring.start()

    turns[0][0].start()
    turns[0][1].start()
    turns[0][0].forward()
    for step in range(1, TERMS):
        turns[step - 1][0].middle()
        turns[step - 1][1].forward()
        finish(step, 0)
        turns[step - 1][1].middle()
        if step < TERMS - 1:
            turns[step][0].forward()
        finish(step, 1)

    get_t.s2()
    get_t.s3()
    get_t.s4()
    get_t.done()
    for k in range(4):
        units[pl.ds(48 * k, 48)] = colt[k].reshape(TC, 768).T.reshape(48, 16, TC)

    for b in range(RB):
        for h in range(2):
            own(4)[pl.ds(BLK * b + 16 * h, 16), :] = units[2 * order[r * RB + b] + h]
    row_t = Rows(4)
    row_t.start()
    row_t.forward()
    acc[...] = jnp.zeros_like(acc)

    def accumulate(k):
        left = rows[4, :, pl.ds(pl.multiple_of(k * 768, 768), 768)]
        right = jnp.concatenate([units[2 * order[24 * k + b] + h] for b in range(24) for h in range(2)], axis=0)
        acc[...] += mm(left, right)

    net.wait(row_t.ends[0])
    accumulate(x)
    row_t.near()
    net.wait(row_t.ends[1])
    accumulate(lax.rem(x + 1, 4))
    row_t.far()
    accumulate(lax.rem(x + 3, 4))
    net.wait(row_t.ends[2])
    accumulate(lax.rem(x + 2, 4))
    value = (acc[...] * masks[3].astype(F32)).astype(BF)
    own(5)[...] = value
    colz[y, z] = value
    row_z, get_z = Rows(5), columns(colz)
    get_z.s1()
    row_z.start()
    get_z.s2()
    row_z.forward()
    get_z.s3()
    row_z.near()
    get_z.s4()
    row_z.far()
    row_z.done()
    get_z.done()
    product(5, colz)
    out[...] = (acc[...] * masks[4].astype(F32)).astype(BF)
    net.finish()
    assert net.used <= SEMS, net.used


def on_device(fock, density, margin, fills, firsts, owner_order, seconds):
    vmem = pl.BlockSpec(memory_space=pltpu.VMEM)
    panel = pltpu.VMEM((4, 4, TR, TC), BF)
    return pl.pallas_call(
        body,
        out_shape=jax.ShapeDtypeStruct((TR, TC), BF),
        in_specs=[vmem] * 6 + [pl.BlockSpec(memory_space=pltpu.SMEM)],
        out_specs=vmem,
        scratch_shapes=[
            panel,
            pltpu.VMEM((4, 4, TR + 16, TC), BF),
            panel,
            pltpu.VMEM((4, 4, 96, 768), BF),
            panel,
            pltpu.VMEM((4, 4, TR, 768), BF),
            pltpu.VMEM((TERMS, 4, 96, 768), BF),
            pltpu.VMEM((192, 16, TC), BF),
            pltpu.VMEM((6, TR, N), BF),
            pltpu.VMEM((TR, TC), F32),
            pltpu.VMEM((5, TR, TC), BF),
            pltpu.VMEM((6, 96, 768), BF),
            pltpu.VMEM((256, 768), F32),
            pltpu.SemaphoreType.DMA((SEMS,)),
        ],
        compiler_params=pltpu.CompilerParams(
            collective_id=0, has_side_effects=True, vmem_limit_bytes=60 * 1024 * 1024
        ),
    )(fock, density, margin, fills, firsts, jnp.swapaxes(seconds, 0, 1), owner_order)


def solution(mesh):
    return jax.shard_map(
        on_device,
        mesh=mesh,
        in_specs=(
            P("row", "col"),
            P("row", "col"),
            P("row", "col"),
            P(None, "row", "col"),
            P(None, "row", "col"),
            P(),
            P(None, "row", "col"),
        ),
        out_specs=P("row", "col"),
        check_vma=False,
    )
```

```python
import jax
import jax.numpy as jnp
from jax import lax
from jax.experimental import pallas as pl
from jax.experimental.pallas import tpu as pltpu
from jax.sharding import PartitionSpec as P

MESH = pl.DeviceIdType.MESH
BLK = 32
TERMS = 6
RB = 6
CB = 12
TR = 192
TC = 384
N = 3072
NB = 96
SEMS = 154
BF = jnp.bfloat16
F32 = jnp.float32


def iota(shape, axis):
    return lax.broadcasted_iota(jnp.int32, shape, axis)


def mm(a, b):
    return jnp.dot(a, b, preferred_element_type=F32)


class Net:
    def __init__(self, sems, units):
        self.sems, self.units, self.used, self.groups = sems, units, 0, []
        self.spare, self.taken = [], []

    def sem(self):
        if self.spare:
            made = self.spare.pop(0)
        else:
            made = self.used
            self.used += 1
        self.taken.append(made)
        return self.sems.at[made]

    def release(self, owner):
        for sent in owner.sends:
            self.wait(sent)
            self.groups = [made for made in self.groups if made is not sent]
        self.spare.extend(owner.held)

    def group(self):
        made = [self.sem(), 0]
        return made

    def senders(self):
        made = self.group()
        self.groups.append(made)
        return made

    def copy(self, ref, device, sent, size, got=None, target=None):
        if got is None:
            got = self.sem()
        elif isinstance(got, list):
            got[1] += size
            got = got[0]
        sent[1] += size
        return pltpu.make_async_remote_copy(
            ref, ref if target is None else target, sent[0], got, device_id=device, device_id_type=MESH
        )

    def wait(self, group):
        ref = self.units.at[pl.ds(0, group[1])]
        pltpu.make_async_copy(ref, ref, group[0]).wait()

    def finish(self):
        for made in self.groups:
            self.wait(made)


class Ring:
    def __init__(self, net, k, nexts, piece, sizes, sent, near=None, far=None):
        after, before = nexts
        p = lambda step, part: piece(lax.rem(k + step + 4, 4), part)
        c = lambda step, part, device, got=None: net.copy(p(step, part), device, sent, sizes[part], got)
        self.a0, self.b1 = c(0, 0, after), c(0, 1, before)
        self.a1, self.b0 = c(0, 1, after, near), c(0, 0, before, near)
        self.f0, self.f1 = c(-1, 0, after, far), c(1, 1, before, far)

    def start(self):
        for made in (self.a0, self.b1, self.a1, self.b0):
            made.start()

    def forward(self):
        self.a0.wait_recv()
        self.f0.start()
        self.b1.wait_recv()
        self.f1.start()

    def near(self):
        self.a1.wait_recv()
        self.b0.wait_recv()

    def far(self):
        self.f0.wait_recv()
        self.f1.wait_recv()


class Plane:
    def __init__(self, net, k1, next1, k2, next2, piece_a, piece_b, sizes_a, sizes_b):
        self.net = net
        net.taken = []
        sends = [net.senders(), net.senders()]
        turn = lambda k, s: lax.rem(k + s + 4, 4)
        steps = (0, -1, 1, 2)
        self.ends = []

        def second(k, nexts, piece, sizes, sent):
            rings = []
            for s in steps:
                end = net.group()
                self.ends.append(end)
                rings.append(Ring(net, k, nexts, piece(s), sizes, sent, end, end))
            return rings

        self.a1 = Ring(net, k1, next1, lambda k, p: piece_a(k, k2, p), sizes_a, sends[0])
        self.a2 = second(k2, next2, lambda s: lambda k, p: piece_a(turn(k1, s), k, p), sizes_a, sends[0])
        self.b1 = Ring(net, k2, next2, lambda k, p: piece_b(k1, k, p), sizes_b, sends[1])
        self.b2 = second(k1, next1, lambda s: lambda k, p: piece_b(k, turn(k2, s), p), sizes_b, sends[1])
        self.sends, self.held = sends, net.taken

    def s1(self):
        self.a1.start()
        self.b1.start()
        self.a2[0].start()
        self.b2[0].start()

    def s2(self):
        self.a1.forward()
        self.b1.forward()
        for first, rings in ((self.a1, self.a2), (self.b1, self.b2)):
            first.near()
            rings[1].start()
            rings[2].start()

    def s3(self):
        self.a2[0].forward()
        self.b2[0].forward()
        for first, rings in ((self.a1, self.a2), (self.b1, self.b2)):
            first.far()
            rings[3].start()

    def s4(self):
        for number in (1, 2, 3):
            self.a2[number].forward()
            self.b2[number].forward()

    def end(self, number):
        self.net.wait(self.ends[number])

    def done(self):
        for number in range(8):
            self.end(number)


def body(
    fock, density, margin, fills, firsts, seconds, order, out,
    colp, cols_, colf, colt, colz, panel, series, units, rows, acc, masks, filters, place, across, sems,
):
    r, c = lax.axis_index("row"), lax.axis_index("col")
    y, z = r // 4, lax.rem(r, 4)
    x, core = c // 2, lax.rem(c, 2)
    net = Net(sems, units)

    def dev(yy, zz, xx):
        return (lax.rem(yy + 4, 4) * 4 + lax.rem(zz + 4, 4), lax.rem(xx + 4, 4) * 2 + core)

    next_y = (dev(y + 1, z, x), dev(y - 1, z, x))
    next_z = (dev(y, z + 1, x), dev(y, z - 1, x))
    next_x = (dev(y, z, x + 1), dev(y, z, x - 1))
    sibling = (r, 2 * x + 1 - core)

    barrier = pltpu.get_barrier_semaphore()
    for device in next_y + next_z + next_x + (sibling,):
        pl.semaphore_signal(barrier, inc=1, device_id=device, device_id_type=MESH)
    pl.semaphore_wait(barrier, 7)

    def columns(buf, extra=0):
        parts = ((0, 48), (48, 48)), ((96, 48), (144, 48 + extra))
        piece = lambda cut: lambda k1, k2, p: buf.at[k2, k1, pl.ds(*cut[p]), :]
        sizes = [[size // 16 for _, size in cut] for cut in parts]
        return Plane(net, z, next_z, y, next_y, piece(parts[0]), piece(parts[1]), *sizes)

    class Rows:
        def __init__(self, number):
            net.taken = []
            sent = net.senders()
            piece = lambda k, p: rows.at[number, pl.ds(96 * p, 96), pl.ds((2 * k + core) * TC, TC)]
            self.ring = Ring(net, x, next_x, piece, (6, 6), sent)
            self.ends = [net.group(), net.group(), net.group()]
            turn = lambda s: lax.rem(x + s + 4, 4)
            give = lambda s, p, end: net.copy(piece(turn(s), p), sibling, sent, 6, self.ends[end])
            self.own = (give(0, 0, 0), give(0, 1, 0))
            self.nears = (give(-1, 0, 1), give(1, 1, 1), give(-1, 1, 1), give(1, 0, 1))
            self.fars = (give(2, 0, 2), give(2, 1, 2))
            self.sends, self.held = [sent], net.taken

        def start(self):
            self.ring.start()
            for made in self.own:
                made.start()

        def forward(self):
            ring = self.ring
            for got, further, give in ((ring.a0, ring.f0, 0), (ring.b1, ring.f1, 1)):
                got.wait_recv()
                further.start()
                self.nears[give].start()

        def near(self):
            for got, give in ((self.ring.a1, 2), (self.ring.b0, 3)):
                got.wait_recv()
                self.nears[give].start()

        def far(self):
            for got, give in ((self.ring.f0, 0), (self.ring.f1, 1)):
                got.wait_recv()
                self.fars[give].start()

        def done(self):
            for end in self.ends:
                net.wait(end)

    spread_rows = (iota((TR, RB), 0) // BLK == iota((TR, RB), 1)).astype(BF)
    spread_cols = (iota((CB, TC), 0) == iota((CB, TC), 1) // BLK).astype(BF)

    def expand(mask):
        wide = mm(mask.astype(F32).astype(BF), spread_cols).astype(BF)
        return mm(spread_rows, wide)

    def own(number):
        return rows.at[number, :, pl.ds(pl.multiple_of(c * TC, TC), TC)]

    def product(number, buf, sign=0):
        if not sign:
            acc[...] = jnp.zeros_like(acc)

        @pl.loop(0, 4)
        def _(k):
            left = rows[number, :, pl.ds(pl.multiple_of(k * 768, 768), 768)]
            right = buf[k, :, pl.ds(0, TR), :].reshape(768, TC)
            if sign:
                acc[...] -= mm(left, right)
            else:
                acc[...] += mm(left, right)

    colp[y, z] = (density[...].astype(F32) * expand(fills[1])).astype(BF)
    get_p = columns(colp)
    get_p.s1()
    row_f, row_s, row_g, row_h = [Rows(number) for number in range(4)]
    masked = (fock[...].astype(F32) * expand(fills[0])).astype(BF)
    own(0)[...] = masked
    row_f.start()
    colf[y, z] = masked
    masked = (margin[...].astype(F32) * expand(fills[2])).astype(BF)
    own(1)[...] = masked
    row_s.start()
    cols_[y, z, pl.ds(0, TR), :] = masked
    get_s, get_f = columns(cols_, 16), columns(colf)
    get_p.s2()
    row_f.forward()
    packed = jnp.zeros((16, TC), F32)
    pad16 = (iota((16, RB), 0) == iota((16, RB), 1)).astype(BF)
    for number in range(TERMS - 1):
        shift = (iota((CB, TC), 1) == CB * number + iota((CB, TC), 0)).astype(BF)
        packed += mm(mm(pad16, seconds[:, number, :].astype(F32).astype(BF)).astype(BF), shift)
    cols_[y, z, pl.ds(TR, 16), :] = packed.astype(BF)
    get_p.s3()
    row_f.near()
    row_s.forward()
    for number in range(3):
        masks[number] = expand(firsts[number]).astype(BF)
    get_p.s4()
    get_s.s1()
    row_f.far()
    row_s.near()
    row_s.far()
    row_f.done()
    get_p.done()
    get_s.s2()
    product(0, colp)
    own(2)[...] = (acc[...] * masks[0].astype(F32)).astype(BF)
    row_g.start()
    row_s.done()
    get_s.s3()
    product(1, colp)
    own(3)[...] = (acc[...] * masks[1].astype(F32)).astype(BF)
    row_h.start()
    get_s.s4()
    get_f.s1()
    row_g.forward()
    row_g.near()
    row_h.forward()
    net.release(get_p)
    net.release(row_f)
    net.release(row_s)
    column_block = 24 * y + iota((1, 768), 1) // BLK
    place[...] = jnp.zeros_like(place)

    @pl.loop(0, 16)
    def _(k):
        for i in range(RB):
            place[pl.ds(16 * k + i, 1), :] = (column_block == order[RB * k + i]).astype(F32)

    base = CB * c + 3 * z
    same = lax.rem(iota((BLK, 768), 0), BLK) == lax.rem(iota((BLK, 768), 1), BLK)
    for i in range(3):
        mine = order[base + i]
        for k in range(4):
            hit = jnp.logical_and(same, iota((BLK, 768), 1) // BLK + 24 * k == mine)
            series[0, k, pl.ds(BLK * i, BLK), :] = hit.astype(F32).astype(BF)
        hit = jnp.logical_and(same, iota((BLK, 768), 1) // BLK + 24 * y == mine)
        filters[5, pl.ds(BLK * i, BLK), :] = hit.astype(F32).astype(BF)
    masks[3] = expand(seconds[:, TERMS - 1, :]).astype(BF)
    masks[4] = expand(seconds[:, TERMS, :]).astype(BF)
    get_s.done()
    get_f.s2()
    row_g.far()
    row_h.near()
    get_f.s3()
    row_h.far()
    row_g.done()
    get_f.s4()
    known = cols_[:, :, pl.ds(TR, 16), :].reshape(256, TC)
    spread = iota((TC, 96), 0) - 3 * z
    for number in range(TERMS - 1):
        pick = (spread == CB * number + iota((TC, 96), 1) // BLK).astype(BF)
        wide = mm(known, pick).astype(BF)
        filters[number] = lax.dot_general(
            wide, place[...].astype(BF), (((0,), (0,)), ((), ())), preferred_element_type=F32
        ).astype(BF)
    product(2, cols_)
    row_h.done()
    get_f.done()
    product(3, colf, -1)
    net.release(get_s)
    net.release(get_f)
    net.release(row_g)
    net.release(row_h)

    tile = (acc[...] * masks[2].astype(F32)).astype(BF)
    side = pl.ds(pl.multiple_of(core * TC, TC), TC)
    panel[x, z, :, side] = (tile.astype(F32) * 0.25).astype(BF)
    cut = lambda base: lambda k1, k2, p: panel.at[k2, k1, pl.ds(base + 48 * p, 48), side]
    get_x = Plane(net, z, next_z, x, next_x, cut(0), cut(96), (3, 3), (3, 3))
    get_x.s1()
    sent, pairs, end = net.senders(), [], net.group()
    for s in (0, -1, 1, 2):
        ref = panel.at[:, lax.rem(z + s + 4, 4), pl.ds(0, 96), side]
        pairs.append(net.copy(ref, sibling, sent, 24, end))
    for s in (0, -1, 1, 2):
        ref = panel.at[lax.rem(x + s + 4, 4), :, pl.ds(96, 96), side]
        pairs.append(net.copy(ref, sibling, sent, 24, end))
    get_x.s2()
    get_x.s3()
    get_x.s4()
    for number in (0, 4, 1, 2, 5, 6, 3, 7):
        get_x.end(number)
        pairs[number].start()
    net.wait(end)
    net.release(get_x)

    def piece_times(step, k, half):
        left = series[step, k] if half is None else series[step, k, pl.ds(48 * half, 48), :]
        return mm(left, across[k])

    def filtered(step, half, total):
        cut = pl.ds(0, 96) if half is None else pl.ds(48 * half, 48)
        eye = filters[5, cut, :].astype(F32)
        if step == 0:
            return eye + total / float(TERMS)
        return eye + total * filters[step - 1, cut, :].astype(F32) / float(TERMS - step)

    class Turn:
        def __init__(self, step, half):
            self.step, self.half = step, half
            self.near, self.far = net.group(), net.group()
            piece = lambda k, p: series.at[step, k, pl.ds(48 * half, 48), pl.ds(TC * p, TC)]
            self.ring = Ring(net, y, next_y, piece, (3, 3), net.senders(), self.near, self.far)

        def start(self):
            self.ring.start()
            sums[self.half] = piece_times(self.step, y, self.half)

        def forward(self):
            self.ring.forward()

        def middle(self):
            net.wait(self.near)
            for s in (-1, 1):
                sums[self.half] += piece_times(self.step, lax.rem(y + s + 4, 4), self.half)

        def finish(self):
            net.wait(self.far)
            total = sums[self.half] + piece_times(self.step, lax.rem(y + 2, 4), self.half)
            return filtered(self.step, self.half, total)

    sums = {}

    def put(step, half, value):
        series[step, y, pl.ds(48 * half, 48), :] = value.astype(BF)

    turns = [[Turn(step, half) for half in range(2)] for step in range(1, TERMS)]
    total = jnp.zeros((96, 768), F32)
    for k in range(4):
        block = panel[k].reshape(768, 768).T
        across[k] = block
        total += mm(series[0, k], block)
    series[1, y] = filtered(0, None, total).astype(BF)
    cut = lambda base: lambda k1, k2, p: colt.at[k2, k1, pl.ds(base, 48), pl.ds(TC * p, TC)]
    get_t = Plane(net, z, next_z, y, next_y, cut(0), cut(48), (3, 3), (3, 3))

    def finish(step, half):
        value = turns[step - 1][half].finish()
        if step < TERMS - 1:
            put(step + 1, half, value)
            turns[step][half].start()
        else:
            colt[y, z, pl.ds(48 * half, 48), :] = value.astype(BF)
            for ring in ((get_t.a1, get_t.a2[0]), (get_t.b1, get_t.b2[0]))[half]:
                ring.start()

    turns[0][0].start()
    turns[0][1].start()
    for step in range(1, TERMS):
        for half in range(2):
            turns[step - 1][half].forward()
        for half in range(2):
            turns[step - 1][half].middle()
            finish(step, half)

    get_t.s2()
    get_t.s3()
    get_t.s4()
    get_t.done()
    for k in range(4):
        units[pl.ds(48 * k, 48)] = colt[k].reshape(TC, 768).T.reshape(48, 16, TC)

    for b in range(RB):
        for h in range(2):
            own(4)[pl.ds(BLK * b + 16 * h, 16), :] = units[2 * order[r * RB + b] + h]
    row_t = Rows(4)
    row_t.start()

    @pl.loop(0, 4)
    def _(k):
        for b in range(24):
            for h in range(2):
                colf[k, b // 6, pl.ds(BLK * (b % 6) + 16 * h, 16), :] = units[2 * order[24 * k + b] + h]

    row_t.forward()
    acc[...] = jnp.zeros_like(acc)

    def accumulate(k):
        left = rows[4, :, pl.ds(pl.multiple_of(k * 768, 768), 768)]
        acc[...] += mm(left, colf[k].reshape(768, TC))

    net.wait(row_t.ends[0])
    accumulate(x)
    row_t.near()
    net.wait(row_t.ends[1])
    accumulate(lax.rem(x + 1, 4))
    row_t.far()
    accumulate(lax.rem(x + 3, 4))
    net.wait(row_t.ends[2])
    accumulate(lax.rem(x + 2, 4))
    value = (acc[...] * masks[3].astype(F32)).astype(BF)
    own(5)[...] = value
    colz[y, z] = value
    row_z, get_z = Rows(5), columns(colz)
    get_z.s1()
    row_z.start()
    get_z.s2()
    row_z.forward()
    get_z.s3()
    row_z.near()
    get_z.s4()
    row_z.far()
    row_z.done()
    get_z.done()
    product(5, colz)
    out[...] = (acc[...] * masks[4].astype(F32)).astype(BF)
    net.finish()
    assert net.used <= SEMS, net.used


def on_device(fock, density, margin, fills, firsts, owner_order, seconds):
    vmem = pl.BlockSpec(memory_space=pltpu.VMEM)
    panel = pltpu.VMEM((4, 4, TR, TC), BF)
    return pl.pallas_call(
        body,
        out_shape=jax.ShapeDtypeStruct((TR, TC), BF),
        in_specs=[vmem] * 6 + [pl.BlockSpec(memory_space=pltpu.SMEM)],
        out_specs=vmem,
        scratch_shapes=[
            panel,
            pltpu.VMEM((4, 4, TR + 16, TC), BF),
            panel,
            pltpu.VMEM((4, 4, 96, 768), BF),
            panel,
            pltpu.VMEM((4, 4, TR, 768), BF),
            pltpu.VMEM((TERMS, 4, 96, 768), BF),
            pltpu.VMEM((192, 16, TC), BF),
            pltpu.VMEM((6, TR, N), BF),
            pltpu.VMEM((TR, TC), F32),
            pltpu.VMEM((5, TR, TC), BF),
            pltpu.VMEM((6, 96, 768), BF),
            pltpu.VMEM((256, 768), F32),
            pltpu.VMEM((4, 768, 768), BF),
            pltpu.SemaphoreType.DMA((SEMS,)),
        ],
        compiler_params=pltpu.CompilerParams(
            collective_id=0, has_side_effects=True, vmem_limit_bytes=60 * 1024 * 1024
        ),
    )(fock, density, margin, fills, firsts, jnp.swapaxes(seconds, 0, 1), owner_order)


def solution(mesh):
    return jax.shard_map(
        on_device,
        mesh=mesh,
        in_specs=(
            P("row", "col"),
            P("row", "col"),
            P("row", "col"),
            P(None, "row", "col"),
            P(None, "row", "col"),
            P(),
            P(None, "row", "col"),
        ),
        out_specs=P("row", "col"),
        check_vma=False,
    )
```

```python
import jax
import jax.numpy as jnp
from jax import lax
from jax.experimental import pallas as pl
from jax.experimental.pallas import tpu as pltpu
from jax.sharding import PartitionSpec as P

MESH = pl.DeviceIdType.MESH
BLK = 32
TERMS = 6
RB = 6
CB = 12
TR = 192
TC = 384
N = 3072
NB = 96
SEMS = 154
BF = jnp.bfloat16
F32 = jnp.float32


def iota(shape, axis):
    return lax.broadcasted_iota(jnp.int32, shape, axis)


def mm(a, b):
    return jnp.dot(a, b, preferred_element_type=F32)


class Net:
    def __init__(self, sems, units):
        self.sems, self.units, self.used, self.groups = sems, units, 0, []
        self.spare, self.taken = [], []

    def sem(self):
        if self.spare:
            made = self.spare.pop(0)
        else:
            made = self.used
            self.used += 1
        self.taken.append(made)
        return self.sems.at[made]

    def release(self, owner):
        for sent in owner.sends:
            self.wait(sent)
            self.groups = [made for made in self.groups if made is not sent]
        self.spare.extend(owner.held)

    def group(self):
        made = [self.sem(), 0]
        return made

    def senders(self):
        made = self.group()
        self.groups.append(made)
        return made

    def copy(self, ref, device, sent, size, got=None, target=None):
        if got is None:
            got = self.sem()
        elif isinstance(got, list):
            got[1] += size
            got = got[0]
        sent[1] += size
        return pltpu.make_async_remote_copy(
            ref, ref if target is None else target, sent[0], got, device_id=device, device_id_type=MESH
        )

    def wait(self, group):
        ref = self.units.at[pl.ds(0, group[1])]
        pltpu.make_async_copy(ref, ref, group[0]).wait()

    def finish(self):
        for made in self.groups:
            self.wait(made)


class Ring:
    def __init__(self, net, k, nexts, piece, sizes, sent, near=None, far=None):
        after, before = nexts
        p = lambda step, part: piece(lax.rem(k + step + 4, 4), part)
        c = lambda step, part, device, got=None: net.copy(p(step, part), device, sent, sizes[part], got)
        self.a0, self.b1 = c(0, 0, after), c(0, 1, before)
        self.a1, self.b0 = c(0, 1, after, near), c(0, 0, before, near)
        self.f0, self.f1 = c(-1, 0, after, far), c(1, 1, before, far)

    def start(self):
        for made in (self.a0, self.b1, self.a1, self.b0):
            made.start()

    def forward(self):
        self.a0.wait_recv()
        self.f0.start()
        self.b1.wait_recv()
        self.f1.start()

    def near(self):
        self.a1.wait_recv()
        self.b0.wait_recv()

    def far(self):
        self.f0.wait_recv()
        self.f1.wait_recv()


class Plane:
    def __init__(self, net, k1, next1, k2, next2, piece_a, piece_b, sizes_a, sizes_b, fine=False):
        self.net = net
        net.taken = []
        sends = [net.senders(), net.senders()]
        turn = lambda k, s: lax.rem(k + s + 4, 4)
        steps = (0, -1, 1, 2)
        self.ends = []

        def second(k, nexts, piece, sizes, sent):
            rings = []
            for s in steps:
                near = net.group()
                far = net.group() if fine and s == 2 else near
                self.ends.append((near, far))
                rings.append(Ring(net, k, nexts, piece(s), sizes, sent, near, far))
            return rings

        self.a1 = Ring(net, k1, next1, lambda k, p: piece_a(k, k2, p), sizes_a, sends[0])
        self.a2 = second(k2, next2, lambda s: lambda k, p: piece_a(turn(k1, s), k, p), sizes_a, sends[0])
        self.b1 = Ring(net, k2, next2, lambda k, p: piece_b(k1, k, p), sizes_b, sends[1])
        self.b2 = second(k1, next1, lambda s: lambda k, p: piece_b(k, turn(k2, s), p), sizes_b, sends[1])
        self.sends, self.held = sends, net.taken

    def s1(self):
        self.a1.start()
        self.b1.start()
        self.a2[0].start()
        self.b2[0].start()

    def s2(self):
        self.a1.forward()
        self.b1.forward()
        for first, rings in ((self.a1, self.a2), (self.b1, self.b2)):
            first.near()
            rings[1].start()
            rings[2].start()

    def s3(self):
        self.a2[0].forward()
        self.b2[0].forward()
        for first, rings in ((self.a1, self.a2), (self.b1, self.b2)):
            first.far()
            rings[3].start()

    def s4(self):
        for number in (1, 2, 3):
            self.a2[number].forward()
            self.b2[number].forward()

    def end(self, number):
        self.net.wait(self.ends[number][0])

    def done(self):
        for number in range(8):
            self.end(number)


def body(
    fock, density, margin, fills, firsts, seconds, order, out,
    colp, cols_, colf, colt, colz, panel, series, units, rows, acc, masks, filters, place, across, sems,
):
    r, c = lax.axis_index("row"), lax.axis_index("col")
    y, z = r // 4, lax.rem(r, 4)
    x, core = c // 2, lax.rem(c, 2)
    net = Net(sems, units)

    def dev(yy, zz, xx):
        return (lax.rem(yy + 4, 4) * 4 + lax.rem(zz + 4, 4), lax.rem(xx + 4, 4) * 2 + core)

    next_y = (dev(y + 1, z, x), dev(y - 1, z, x))
    next_z = (dev(y, z + 1, x), dev(y, z - 1, x))
    next_x = (dev(y, z, x + 1), dev(y, z, x - 1))
    sibling = (r, 2 * x + 1 - core)

    barrier = pltpu.get_barrier_semaphore()
    for device in next_y + next_z + next_x + (sibling,):
        pl.semaphore_signal(barrier, inc=1, device_id=device, device_id_type=MESH)

    def columns(buf, extra=0):
        parts = ((0, 48), (48, 48)), ((96, 48), (144, 48 + extra))
        piece = lambda cut: lambda k1, k2, p: buf.at[k2, k1, pl.ds(*cut[p]), :]
        sizes = [[size // 16 for _, size in cut] for cut in parts]
        return Plane(net, z, next_z, y, next_y, piece(parts[0]), piece(parts[1]), *sizes)

    class Rows:
        def __init__(self, number):
            net.taken = []
            sent = net.senders()
            piece = lambda k, p: rows.at[number, pl.ds(96 * p, 96), pl.ds((2 * k + core) * TC, TC)]
            self.ring = Ring(net, x, next_x, piece, (6, 6), sent)
            self.ends = [net.group(), net.group(), net.group()]
            turn = lambda s: lax.rem(x + s + 4, 4)
            give = lambda s, p, end: net.copy(piece(turn(s), p), sibling, sent, 6, self.ends[end])
            self.own = (give(0, 0, 0), give(0, 1, 0))
            self.nears = (give(-1, 0, 1), give(1, 1, 1), give(-1, 1, 1), give(1, 0, 1))
            self.fars = (give(2, 0, 2), give(2, 1, 2))
            self.sends, self.held = [sent], net.taken

        def start(self):
            self.ring.start()
            for made in self.own:
                made.start()

        def forward(self):
            ring = self.ring
            for got, further, give in ((ring.a0, ring.f0, 0), (ring.b1, ring.f1, 1)):
                got.wait_recv()
                further.start()
                self.nears[give].start()

        def near(self):
            for got, give in ((self.ring.a1, 2), (self.ring.b0, 3)):
                got.wait_recv()
                self.nears[give].start()

        def far(self):
            for got, give in ((self.ring.f0, 0), (self.ring.f1, 1)):
                got.wait_recv()
                self.fars[give].start()

        def done(self):
            for end in self.ends:
                net.wait(end)

    spread_rows = (iota((TR, RB), 0) // BLK == iota((TR, RB), 1)).astype(BF)
    spread_cols = (iota((CB, TC), 0) == iota((CB, TC), 1) // BLK).astype(BF)

    def expand(mask):
        wide = mm(mask.astype(F32).astype(BF), spread_cols).astype(BF)
        return mm(spread_rows, wide)

    def own(number):
        return rows.at[number, :, pl.ds(pl.multiple_of(c * TC, TC), TC)]

    def product(number, buf, sign=0):
        if not sign:
            acc[...] = jnp.zeros_like(acc)

        @pl.loop(0, 4)
        def _(k):
            left = rows[number, :, pl.ds(pl.multiple_of(k * 768, 768), 768)]
            right = buf[k, :, pl.ds(0, TR), :].reshape(768, TC)
            if sign:
                acc[...] -= mm(left, right)
            else:
                acc[...] += mm(left, right)

    colp[y, z] = (density[...].astype(F32) * expand(fills[1])).astype(BF)
    masked = (fock[...].astype(F32) * expand(fills[0])).astype(BF)
    own(0)[...] = masked
    colf[y, z] = masked
    pl.semaphore_wait(barrier, 7)
    get_p = columns(colp)
    get_p.s1()
    row_f, row_s, row_g, row_h = [Rows(number) for number in range(4)]
    row_f.start()
    masked = (margin[...].astype(F32) * expand(fills[2])).astype(BF)
    own(1)[...] = masked
    row_s.start()
    cols_[y, z, pl.ds(0, TR), :] = masked
    get_s, get_f = columns(cols_, 16), columns(colf)
    get_p.s2()
    row_f.forward()
    packed = jnp.zeros((16, TC), F32)
    pad16 = (iota((16, RB), 0) == iota((16, RB), 1)).astype(BF)
    for number in range(TERMS - 1):
        shift = (iota((CB, TC), 1) == CB * number + iota((CB, TC), 0)).astype(BF)
        packed += mm(mm(pad16, seconds[:, number, :].astype(F32).astype(BF)).astype(BF), shift)
    cols_[y, z, pl.ds(TR, 16), :] = packed.astype(BF)
    get_p.s3()
    row_f.near()
    row_s.forward()
    for number in range(3):
        masks[number] = expand(firsts[number]).astype(BF)
    get_p.s4()
    get_s.s1()
    row_f.far()
    row_s.near()
    row_s.far()
    row_f.done()
    get_p.done()
    get_s.s2()
    product(0, colp)
    own(2)[...] = (acc[...] * masks[0].astype(F32)).astype(BF)
    row_g.start()
    row_s.done()
    get_s.s3()
    product(1, colp)
    own(3)[...] = (acc[...] * masks[1].astype(F32)).astype(BF)
    row_h.start()
    get_s.s4()
    get_f.s1()
    row_g.forward()
    row_g.near()
    row_h.forward()
    net.release(get_p)
    net.release(row_f)
    net.release(row_s)
    column_block = 24 * y + iota((1, 768), 1) // BLK
    place[...] = jnp.zeros_like(place)

    @pl.loop(0, 16)
    def _(k):
        for i in range(RB):
            place[pl.ds(16 * k + i, 1), :] = (column_block == order[RB * k + i]).astype(F32)

    base = CB * c + 3 * z
    same = lax.rem(iota((BLK, 768), 0), BLK) == lax.rem(iota((BLK, 768), 1), BLK)
    for i in range(3):
        mine = order[base + i]
        for k in range(4):
            hit = jnp.logical_and(same, iota((BLK, 768), 1) // BLK + 24 * k == mine)
            series[0, k, pl.ds(BLK * i, BLK), :] = hit.astype(F32).astype(BF)
        hit = jnp.logical_and(same, iota((BLK, 768), 1) // BLK + 24 * y == mine)
        filters[5, pl.ds(BLK * i, BLK), :] = hit.astype(F32).astype(BF)
    masks[3] = expand(seconds[:, TERMS - 1, :]).astype(BF)
    masks[4] = expand(seconds[:, TERMS, :]).astype(BF)
    get_s.done()
    get_f.s2()
    row_g.far()
    row_h.near()
    get_f.s3()
    row_h.far()
    row_g.done()
    get_f.s4()
    known = cols_[:, :, pl.ds(TR, 16), :].reshape(256, TC)
    spread = iota((TC, 96), 0) - 3 * z
    for number in range(TERMS - 1):
        pick = (spread == CB * number + iota((TC, 96), 1) // BLK).astype(BF)
        wide = mm(known, pick).astype(BF)
        filters[number] = lax.dot_general(
            wide, place[...].astype(BF), (((0,), (0,)), ((), ())), preferred_element_type=F32
        ).astype(BF)
    product(2, cols_)
    row_h.done()
    get_f.done()
    product(3, colf, -1)
    net.release(get_s)
    net.release(get_f)
    net.release(row_g)
    net.release(row_h)

    tile = (acc[...] * masks[2].astype(F32)).astype(BF)
    side = pl.ds(pl.multiple_of(core * TC, TC), TC)
    panel[x, z, :, side] = (tile.astype(F32) * 0.25).astype(BF)
    cut = lambda base: lambda k1, k2, p: panel.at[k2, k1, pl.ds(base + 48 * p, 48), side]
    get_x = Plane(net, z, next_z, x, next_x, cut(0), cut(96), (3, 3), (3, 3), True)
    get_x.s1()
    sent, pairs, end = net.senders(), [], net.group()
    turn = lambda k, s: lax.rem(k + s + 4, 4)
    for s in (0, -1, 1):
        ref = panel.at[:, turn(z, s), pl.ds(0, 96), side]
        pairs.append(net.copy(ref, sibling, sent, 24, end))
    for s in (0, -1, 1):
        ref = panel.at[turn(x, s), :, pl.ds(96, 96), side]
        pairs.append(net.copy(ref, sibling, sent, 24, end))
    tails = [[], []]
    for s in (0, -1, 1, 2):
        ref = panel.at[turn(x, s), turn(z, 2), pl.ds(0, 96), side]
        tails[0].append(net.copy(ref, sibling, sent, 6, end))
        ref = panel.at[turn(x, 2), turn(z, s), pl.ds(96, 96), side]
        tails[1].append(net.copy(ref, sibling, sent, 6, end))
    get_x.s2()
    get_x.s3()
    for tail in tails:
        tail[0].start()
    get_x.s4()
    for number, pair in ((0, 0), (4, 3), (1, 1), (2, 2), (5, 4), (6, 5)):
        get_x.end(number)
        pairs[pair].start()
    for part in range(2):
        for number, tail in ((3, tails[0]), (7, tails[1])):
            net.wait(get_x.ends[number][part])
            for copy in ((tail[1], tail[2]), (tail[3],))[part]:
                copy.start()
    net.wait(end)
    net.release(get_x)

    def piece_times(step, k, half):
        left = series[step, k] if half is None else series[step, k, pl.ds(48 * half, 48), :]
        return mm(left, across[k])

    def filtered(step, half, total):
        cut = pl.ds(0, 96) if half is None else pl.ds(48 * half, 48)
        eye = filters[5, cut, :].astype(F32)
        if step == 0:
            return eye + total / float(TERMS)
        return eye + total * filters[step - 1, cut, :].astype(F32) / float(TERMS - step)

    class Turn:
        def __init__(self, step, half):
            self.step, self.half = step, half
            self.near, self.far = net.group(), net.group()
            piece = lambda k, p: series.at[step, k, pl.ds(48 * half, 48), pl.ds(TC * p, TC)]
            self.ring = Ring(net, y, next_y, piece, (3, 3), net.senders(), self.near, self.far)

        def start(self):
            self.ring.start()
            sums[self.half] = piece_times(self.step, y, self.half)

        def forward(self):
            self.ring.forward()

        def middle(self):
            net.wait(self.near)
            for s in (-1, 1):
                sums[self.half] += piece_times(self.step, lax.rem(y + s + 4, 4), self.half)

        def finish(self):
            net.wait(self.far)
            total = sums[self.half] + piece_times(self.step, lax.rem(y + 2, 4), self.half)
            return filtered(self.step, self.half, total)

    sums = {}

    def put(step, half, value):
        series[step, y, pl.ds(48 * half, 48), :] = value.astype(BF)

    turns = [[Turn(step, half) for half in range(2)] for step in range(1, TERMS)]
    total = jnp.zeros((96, 768), F32)
    for k in range(4):
        block = panel[k].reshape(768, 768).T
        across[k] = block
        total += mm(series[0, k], block)
    series[1, y] = filtered(0, None, total).astype(BF)
    cut = lambda base: lambda k1, k2, p: colt.at[k2, k1, pl.ds(base, 48), pl.ds(TC * p, TC)]
    get_t = Plane(net, z, next_z, y, next_y, cut(0), cut(48), (3, 3), (3, 3))

    def finish(step, half):
        value = turns[step - 1][half].finish()
        if step < TERMS - 1:
            put(step + 1, half, value)
            turns[step][half].start()
        else:
            colt[y, z, pl.ds(48 * half, 48), :] = value.astype(BF)
            for ring in ((get_t.a1, get_t.a2[0]), (get_t.b1, get_t.b2[0]))[half]:
                ring.start()

    turns[0][0].start()
    turns[0][1].start()
    for step in range(1, TERMS):
        for half in range(2):
            turns[step - 1][half].forward()
        for half in range(2):
            turns[step - 1][half].middle()
            finish(step, half)

    get_t.s2()
    get_t.s3()
    get_t.s4()
    get_t.done()
    for k in range(4):
        units[pl.ds(48 * k, 48)] = colt[k].reshape(TC, 768).T.reshape(48, 16, TC)

    for b in range(RB):
        for h in range(2):
            own(4)[pl.ds(BLK * b + 16 * h, 16), :] = units[2 * order[r * RB + b] + h]
    row_t = Rows(4)
    row_t.start()

    @pl.loop(0, 4)
    def _(k):
        for b in range(24):
            for h in range(2):
                colf[k, b // 6, pl.ds(BLK * (b % 6) + 16 * h, 16), :] = units[2 * order[24 * k + b] + h]

    row_t.forward()
    acc[...] = jnp.zeros_like(acc)

    def accumulate(k):
        left = rows[4, :, pl.ds(pl.multiple_of(k * 768, 768), 768)]
        acc[...] += mm(left, colf[k].reshape(768, TC))

    net.wait(row_t.ends[0])
    accumulate(x)
    row_t.near()
    net.wait(row_t.ends[1])
    accumulate(lax.rem(x + 1, 4))
    row_t.far()
    accumulate(lax.rem(x + 3, 4))
    net.wait(row_t.ends[2])
    accumulate(lax.rem(x + 2, 4))
    value = (acc[...] * masks[3].astype(F32)).astype(BF)
    own(5)[...] = value
    colz[y, z] = value
    row_z, get_z = Rows(5), columns(colz)
    get_z.s1()
    row_z.start()
    get_z.s2()
    row_z.forward()
    get_z.s3()
    row_z.near()
    get_z.s4()
    row_z.far()
    row_z.done()
    get_z.done()
    product(5, colz)
    out[...] = (acc[...] * masks[4].astype(F32)).astype(BF)
    net.finish()
    assert net.used <= SEMS, net.used


def on_device(fock, density, margin, fills, firsts, owner_order, seconds):
    vmem = pl.BlockSpec(memory_space=pltpu.VMEM)
    panel = pltpu.VMEM((4, 4, TR, TC), BF)
    return pl.pallas_call(
        body,
        out_shape=jax.ShapeDtypeStruct((TR, TC), BF),
        in_specs=[vmem] * 6 + [pl.BlockSpec(memory_space=pltpu.SMEM)],
        out_specs=vmem,
        scratch_shapes=[
            panel,
            pltpu.VMEM((4, 4, TR + 16, TC), BF),
            panel,
            pltpu.VMEM((4, 4, 96, 768), BF),
            panel,
            pltpu.VMEM((4, 4, TR, 768), BF),
            pltpu.VMEM((TERMS, 4, 96, 768), BF),
            pltpu.VMEM((192, 16, TC), BF),
            pltpu.VMEM((6, TR, N), BF),
            pltpu.VMEM((TR, TC), F32),
            pltpu.VMEM((5, TR, TC), BF),
            pltpu.VMEM((6, 96, 768), BF),
            pltpu.VMEM((256, 768), F32),
            pltpu.VMEM((4, 768, 768), BF),
            pltpu.SemaphoreType.DMA((SEMS,)),
        ],
        compiler_params=pltpu.CompilerParams(
            collective_id=0, has_side_effects=True, vmem_limit_bytes=60 * 1024 * 1024
        ),
    )(fock, density, margin, fills, firsts, jnp.swapaxes(seconds, 0, 1), owner_order)


def solution(mesh):
    return jax.shard_map(
        on_device,
        mesh=mesh,
        in_specs=(
            P("row", "col"),
            P("row", "col"),
            P("row", "col"),
            P(None, "row", "col"),
            P(None, "row", "col"),
            P(),
            P(None, "row", "col"),
        ),
        out_specs=P("row", "col"),
        check_vma=False,
    )
```

```python
import jax
import jax.numpy as jnp
from jax import lax
from jax.experimental import pallas as pl
from jax.experimental.pallas import tpu as pltpu
from jax.sharding import PartitionSpec as P

MESH = pl.DeviceIdType.MESH
BLK = 32
TERMS = 6
RB = 6
CB = 12
TR = 192
TC = 384
N = 3072
NB = 96
SEMS = 154
BF = jnp.bfloat16
F32 = jnp.float32


def iota(shape, axis):
    return lax.broadcasted_iota(jnp.int32, shape, axis)


def mm(a, b):
    return jnp.dot(a, b, preferred_element_type=F32)


class Net:
    def __init__(self, sems, units):
        self.sems, self.units, self.used, self.groups = sems, units, 0, []
        self.spare, self.taken = [], []

    def sem(self):
        if self.spare:
            made = self.spare.pop(0)
        else:
            made = self.used
            self.used += 1
        self.taken.append(made)
        return self.sems.at[made]

    def release(self, owner):
        for sent in owner.sends:
            self.wait(sent)
            self.groups = [made for made in self.groups if made is not sent]
        self.spare.extend(owner.held)

    def group(self):
        made = [self.sem(), 0]
        return made

    def senders(self):
        made = self.group()
        self.groups.append(made)
        return made

    def copy(self, ref, device, sent, size, got=None, target=None):
        if got is None:
            got = self.sem()
        elif isinstance(got, list):
            got[1] += size
            got = got[0]
        sent[1] += size
        return pltpu.make_async_remote_copy(
            ref, ref if target is None else target, sent[0], got, device_id=device, device_id_type=MESH
        )

    def wait(self, group):
        ref = self.units.at[pl.ds(0, group[1])]
        pltpu.make_async_copy(ref, ref, group[0]).wait()

    def finish(self):
        for made in self.groups:
            self.wait(made)


class Ring:
    def __init__(self, net, k, nexts, piece, sizes, sent, near=None, far=None):
        after, before = nexts
        p = lambda step, part: piece(lax.rem(k + step + 4, 4), part)
        c = lambda step, part, device, got=None: net.copy(p(step, part), device, sent, sizes[part], got)
        self.a0, self.b1 = c(0, 0, after), c(0, 1, before)
        self.a1, self.b0 = c(0, 1, after, near), c(0, 0, before, near)
        self.f0, self.f1 = c(-1, 0, after, far), c(1, 1, before, far)

    def start(self):
        for made in (self.a0, self.b1, self.a1, self.b0):
            made.start()

    def forward(self):
        self.a0.wait_recv()
        self.f0.start()
        self.b1.wait_recv()
        self.f1.start()

    def near(self):
        self.a1.wait_recv()
        self.b0.wait_recv()

    def far(self):
        self.f0.wait_recv()
        self.f1.wait_recv()


class Plane:
    def __init__(self, net, k1, next1, k2, next2, piece_a, piece_b, sizes_a, sizes_b, fine=False):
        self.net = net
        net.taken = []
        sends = [net.senders(), net.senders()]
        turn = lambda k, s: lax.rem(k + s + 4, 4)
        steps = (0, -1, 1, 2)
        self.ends = []

        def second(k, nexts, piece, sizes, sent):
            rings = []
            for s in steps:
                near = net.group()
                far = net.group() if fine and s == 2 else near
                self.ends.append((near, far))
                rings.append(Ring(net, k, nexts, piece(s), sizes, sent, near, far))
            return rings

        self.a1 = Ring(net, k1, next1, lambda k, p: piece_a(k, k2, p), sizes_a, sends[0])
        self.a2 = second(k2, next2, lambda s: lambda k, p: piece_a(turn(k1, s), k, p), sizes_a, sends[0])
        self.b1 = Ring(net, k2, next2, lambda k, p: piece_b(k1, k, p), sizes_b, sends[1])
        self.b2 = second(k1, next1, lambda s: lambda k, p: piece_b(k, turn(k2, s), p), sizes_b, sends[1])
        self.sends, self.held = sends, net.taken

    def s1(self):
        self.a1.start()
        self.b1.start()
        self.a2[0].start()
        self.b2[0].start()

    def s2(self):
        self.a1.forward()
        self.b1.forward()
        for first, rings in ((self.a1, self.a2), (self.b1, self.b2)):
            first.near()
            rings[1].start()
            rings[2].start()

    def s3(self):
        self.a2[0].forward()
        self.b2[0].forward()
        for first, rings in ((self.a1, self.a2), (self.b1, self.b2)):
            first.far()
            rings[3].start()

    def s4(self):
        for number in (1, 2, 3):
            self.a2[number].forward()
            self.b2[number].forward()

    def end(self, number):
        self.net.wait(self.ends[number][0])

    def done(self):
        for number in range(8):
            self.end(number)


def body(
    fock, density, margin, fills, firsts, seconds, order, out,
    colp, cols_, colf, colt, colz, panel, series, units, rows, acc, masks, filters, place, across, sems,
):
    r, c = lax.axis_index("row"), lax.axis_index("col")
    y, z = r // 4, lax.rem(r, 4)
    x, core = c // 2, lax.rem(c, 2)
    net = Net(sems, units)

    def dev(yy, zz, xx):
        return (lax.rem(yy + 4, 4) * 4 + lax.rem(zz + 4, 4), lax.rem(xx + 4, 4) * 2 + core)

    next_y = (dev(y + 1, z, x), dev(y - 1, z, x))
    next_z = (dev(y, z + 1, x), dev(y, z - 1, x))
    next_x = (dev(y, z, x + 1), dev(y, z, x - 1))
    sibling = (r, 2 * x + 1 - core)

    barrier = pltpu.get_barrier_semaphore()
    for device in next_y + next_z + next_x + (sibling,):
        pl.semaphore_signal(barrier, inc=1, device_id=device, device_id_type=MESH)

    def columns(buf, extra=0):
        parts = ((0, 48), (48, 48)), ((96, 48), (144, 48 + extra))
        piece = lambda cut: lambda k1, k2, p: buf.at[k2, k1, pl.ds(*cut[p]), :]
        sizes = [[size // 16 for _, size in cut] for cut in parts]
        return Plane(net, z, next_z, y, next_y, piece(parts[0]), piece(parts[1]), *sizes)

    class Rows:
        def __init__(self, number):
            net.taken = []
            sent = net.senders()
            piece = lambda k, p: rows.at[number, pl.ds(96 * p, 96), pl.ds((2 * k + core) * TC, TC)]
            self.ring = Ring(net, x, next_x, piece, (6, 6), sent)
            self.ends = [net.group(), net.group(), net.group()]
            turn = lambda s: lax.rem(x + s + 4, 4)
            give = lambda s, p, end: net.copy(piece(turn(s), p), sibling, sent, 6, self.ends[end])
            self.own = (give(0, 0, 0), give(0, 1, 0))
            self.nears = (give(-1, 0, 1), give(1, 1, 1), give(-1, 1, 1), give(1, 0, 1))
            self.fars = (give(2, 0, 2), give(2, 1, 2))
            self.sends, self.held = [sent], net.taken

        def start(self):
            self.ring.start()
            for made in self.own:
                made.start()

        def forward(self):
            ring = self.ring
            for got, further, give in ((ring.a0, ring.f0, 0), (ring.b1, ring.f1, 1)):
                got.wait_recv()
                further.start()
                self.nears[give].start()

        def near(self):
            for got, give in ((self.ring.a1, 2), (self.ring.b0, 3)):
                got.wait_recv()
                self.nears[give].start()

        def far(self):
            for got, give in ((self.ring.f0, 0), (self.ring.f1, 1)):
                got.wait_recv()
                self.fars[give].start()

        def done(self):
            for end in self.ends:
                net.wait(end)

    spread_rows = (iota((TR, RB), 0) // BLK == iota((TR, RB), 1)).astype(BF)
    spread_cols = (iota((CB, TC), 0) == iota((CB, TC), 1) // BLK).astype(BF)

    def expand(mask):
        wide = mm(mask.astype(F32).astype(BF), spread_cols).astype(BF)
        return mm(spread_rows, wide)

    def own(number):
        return rows.at[number, :, pl.ds(pl.multiple_of(c * TC, TC), TC)]

    def product(number, buf, sign=0):
        if not sign:
            acc[...] = jnp.zeros_like(acc)

        @pl.loop(0, 4)
        def _(k):
            left = rows[number, :, pl.ds(pl.multiple_of(k * 768, 768), 768)]
            right = buf[k, :, pl.ds(0, TR), :].reshape(768, TC)
            if sign:
                acc[...] -= mm(left, right)
            else:
                acc[...] += mm(left, right)

    colp[y, z] = (density[...].astype(F32) * expand(fills[1])).astype(BF)
    masked = (fock[...].astype(F32) * expand(fills[0])).astype(BF)
    own(0)[...] = masked
    colf[y, z] = masked
    pl.semaphore_wait(barrier, 7)
    get_p = columns(colp)
    get_p.s1()
    row_f, row_s, row_g, row_h = [Rows(number) for number in range(4)]
    row_f.start()
    masked = (margin[...].astype(F32) * expand(fills[2])).astype(BF)
    own(1)[...] = masked
    row_s.start()
    cols_[y, z, pl.ds(0, TR), :] = masked
    get_s, get_f = columns(cols_, 16), columns(colf)
    get_p.s2()
    row_f.forward()
    packed = jnp.zeros((16, TC), F32)
    pad16 = (iota((16, RB), 0) == iota((16, RB), 1)).astype(BF)
    for number in range(TERMS - 1):
        shift = (iota((CB, TC), 1) == CB * number + iota((CB, TC), 0)).astype(BF)
        packed += mm(mm(pad16, seconds[:, number, :].astype(F32).astype(BF)).astype(BF), shift)
    cols_[y, z, pl.ds(TR, 16), :] = packed.astype(BF)
    get_p.s3()
    row_f.near()
    row_s.forward()
    for number in range(3):
        masks[number] = expand(firsts[number]).astype(BF)
    get_p.s4()
    get_s.s1()
    row_f.far()
    row_s.near()
    row_s.far()
    row_f.done()
    get_p.done()
    get_s.s2()
    product(0, colp)
    own(2)[...] = (acc[...] * masks[0].astype(F32)).astype(BF)
    row_g.start()
    row_s.done()
    get_s.s3()
    product(1, colp)
    own(3)[...] = (acc[...] * masks[1].astype(F32)).astype(BF)
    row_h.start()
    get_s.s4()
    get_f.s1()
    row_g.forward()
    row_g.near()
    row_h.forward()
    net.release(get_p)
    net.release(row_f)
    net.release(row_s)
    column_block = 24 * y + iota((1, 768), 1) // BLK
    place[...] = jnp.zeros_like(place)

    @pl.loop(0, 16)
    def _(k):
        for i in range(RB):
            place[pl.ds(16 * k + i, 1), :] = (column_block == order[RB * k + i]).astype(F32)

    base = CB * c + 3 * z
    same = lax.rem(iota((BLK, 768), 0), BLK) == lax.rem(iota((BLK, 768), 1), BLK)
    for i in range(3):
        mine = order[base + i]
        for k in range(4):
            hit = jnp.logical_and(same, iota((BLK, 768), 1) // BLK + 24 * k == mine)
            series[0, k, pl.ds(BLK * i, BLK), :] = hit.astype(F32).astype(BF)
        hit = jnp.logical_and(same, iota((BLK, 768), 1) // BLK + 24 * y == mine)
        filters[5, pl.ds(BLK * i, BLK), :] = hit.astype(F32).astype(BF)
    masks[3] = expand(seconds[:, TERMS - 1, :]).astype(BF)
    masks[4] = expand(seconds[:, TERMS, :]).astype(BF)
    get_s.done()
    get_f.s2()
    row_g.far()
    row_h.near()
    get_f.s3()
    row_h.far()
    row_g.done()
    get_f.s4()
    known = cols_[:, :, pl.ds(TR, 16), :].reshape(256, TC)
    spread = iota((TC, 96), 0) - 3 * z
    for number in range(TERMS - 1):
        pick = (spread == CB * number + iota((TC, 96), 1) // BLK).astype(BF)
        wide = mm(known, pick).astype(BF)
        filters[number] = lax.dot_general(
            wide, place[...].astype(BF), (((0,), (0,)), ((), ())), preferred_element_type=F32
        ).astype(BF)
    product(2, cols_)
    row_h.done()
    get_f.done()
    product(3, colf, -1)
    net.release(get_s)
    net.release(get_f)
    net.release(row_g)
    net.release(row_h)

    tile = (acc[...] * masks[2].astype(F32)).astype(BF)
    side = pl.ds(pl.multiple_of(core * TC, TC), TC)
    panel[x, z, :, side] = (tile.astype(F32) * 0.25).astype(BF)
    cut = lambda base: lambda k1, k2, p: panel.at[k2, k1, pl.ds(base + 48 * p, 48), side]
    get_x = Plane(net, z, next_z, x, next_x, cut(0), cut(96), (3, 3), (3, 3), True)
    get_x.s1()
    sent, pairs, end = net.senders(), [], net.group()
    turn = lambda k, s: lax.rem(k + s + 4, 4)
    for s in (0, -1, 1):
        ref = panel.at[:, turn(z, s), pl.ds(0, 96), side]
        pairs.append(net.copy(ref, sibling, sent, 24, end))
    for s in (0, -1, 1):
        ref = panel.at[turn(x, s), :, pl.ds(96, 96), side]
        pairs.append(net.copy(ref, sibling, sent, 24, end))
    tails = [[], []]
    for s in (0, -1, 1, 2):
        ref = panel.at[turn(x, s), turn(z, 2), pl.ds(0, 96), side]
        tails[0].append(net.copy(ref, sibling, sent, 6, end))
        ref = panel.at[turn(x, 2), turn(z, s), pl.ds(96, 96), side]
        tails[1].append(net.copy(ref, sibling, sent, 6, end))
    get_x.s2()
    get_x.s3()
    for tail in tails:
        tail[0].start()
    get_x.s4()
    for number, pair in ((0, 0), (4, 3), (1, 1), (2, 2), (5, 4), (6, 5)):
        get_x.end(number)
        pairs[pair].start()
    for part in range(2):
        for number, tail in ((3, tails[0]), (7, tails[1])):
            net.wait(get_x.ends[number][part])
            for copy in ((tail[1], tail[2]), (tail[3],))[part]:
                copy.start()
    net.wait(end)
    net.release(get_x)

    def piece_times(step, k, half):
        left = series[step, k] if half is None else series[step, k, pl.ds(48 * half, 48), :]
        return mm(left, across[k])

    def filtered(step, half, total):
        cut = pl.ds(0, 96) if half is None else pl.ds(48 * half, 48)
        eye = filters[5, cut, :].astype(F32)
        if step == 0:
            return eye + total / float(TERMS)
        return eye + total * filters[step - 1, cut, :].astype(F32) / float(TERMS - step)

    class Turn:
        def __init__(self, step, half):
            self.step, self.half = step, half
            self.near, self.far = net.group(), net.group()
            piece = lambda k, p: series.at[step, k, pl.ds(48 * half, 48), pl.ds(TC * p, TC)]
            self.ring = Ring(net, y, next_y, piece, (3, 3), net.senders(), self.near, self.far)

        def start(self):
            self.ring.start()

        def forward(self):
            self.ring.forward()

        def middle(self):
            net.wait(self.near)
            for s in (-1, 1):
                sums[self.half] += piece_times(self.step, lax.rem(y + s + 4, 4), self.half)

        def finish(self):
            net.wait(self.far)
            total = sums[self.half] + piece_times(self.step, lax.rem(y + 2, 4), self.half)
            return filtered(self.step, self.half, total)

    sums = {}

    def put(step, half, value):
        series[step, y, pl.ds(48 * half, 48), :] = value.astype(BF)

    turns = [[Turn(step, half) for half in range(2)] for step in range(1, TERMS)]
    total = jnp.zeros((96, 768), F32)
    for k in range(4):
        total += lax.dot_general(
            series[0, k], panel[k].reshape(768, 768), (((1,), (1,)), ((), ())), preferred_element_type=F32
        )
    series[1, y] = filtered(0, None, total).astype(BF)
    cut = lambda base: lambda k1, k2, p: colt.at[k2, k1, pl.ds(base, 48), pl.ds(TC * p, TC)]
    get_t = Plane(net, z, next_z, y, next_y, cut(0), cut(48), (3, 3), (3, 3))

    def finish(step, half):
        value = turns[step - 1][half].finish()
        if step < TERMS - 1:
            put(step + 1, half, value)
            turns[step][half].start()
        else:
            colt[y, z, pl.ds(48 * half, 48), :] = value.astype(BF)
            for ring in ((get_t.a1, get_t.a2[0]), (get_t.b1, get_t.b2[0]))[half]:
                ring.start()

    turns[0][0].start()
    turns[0][1].start()
    for k in range(4):
        across[k] = panel[k].reshape(768, 768).T
    for step in range(1, TERMS):
        for half in range(2):
            turns[step - 1][half].forward()
        own_part = piece_times(step, y, None)
        sums[0], sums[1] = own_part[:48, :], own_part[48:, :]
        for half in range(2):
            turns[step - 1][half].middle()
            finish(step, half)

    get_t.s2()
    get_t.s3()
    get_t.s4()
    get_t.done()
    for k in range(4):
        units[pl.ds(48 * k, 48)] = colt[k].reshape(TC, 768).T.reshape(48, 16, TC)

    for b in range(RB):
        for h in range(2):
            own(4)[pl.ds(BLK * b + 16 * h, 16), :] = units[2 * order[r * RB + b] + h]
    row_t = Rows(4)
    row_t.start()

    @pl.loop(0, 4)
    def _(k):
        for b in range(24):
            for h in range(2):
                colf[k, b // 6, pl.ds(BLK * (b % 6) + 16 * h, 16), :] = units[2 * order[24 * k + b] + h]

    row_t.forward()
    acc[...] = jnp.zeros_like(acc)

    def accumulate(k):
        left = rows[4, :, pl.ds(pl.multiple_of(k * 768, 768), 768)]
        acc[...] += mm(left, colf[k].reshape(768, TC))

    net.wait(row_t.ends[0])
    accumulate(x)
    row_t.near()
    net.wait(row_t.ends[1])
    accumulate(lax.rem(x + 1, 4))
    row_t.far()
    accumulate(lax.rem(x + 3, 4))
    net.wait(row_t.ends[2])
    accumulate(lax.rem(x + 2, 4))
    value = (acc[...] * masks[3].astype(F32)).astype(BF)
    own(5)[...] = value
    colz[y, z] = value
    row_z, get_z = Rows(5), columns(colz)
    get_z.s1()
    row_z.start()
    get_z.s2()
    row_z.forward()
    get_z.s3()
    row_z.near()
    get_z.s4()
    row_z.far()
    row_z.done()
    get_z.done()
    product(5, colz)
    out[...] = (acc[...] * masks[4].astype(F32)).astype(BF)
    net.finish()
    assert net.used <= SEMS, net.used


def on_device(fock, density, margin, fills, firsts, owner_order, seconds):
    vmem = pl.BlockSpec(memory_space=pltpu.VMEM)
    panel = pltpu.VMEM((4, 4, TR, TC), BF)
    return pl.pallas_call(
        body,
        out_shape=jax.ShapeDtypeStruct((TR, TC), BF),
        in_specs=[vmem] * 6 + [pl.BlockSpec(memory_space=pltpu.SMEM)],
        out_specs=vmem,
        scratch_shapes=[
            panel,
            pltpu.VMEM((4, 4, TR + 16, TC), BF),
            panel,
            pltpu.VMEM((4, 4, 96, 768), BF),
            panel,
            pltpu.VMEM((4, 4, TR, 768), BF),
            pltpu.VMEM((TERMS, 4, 96, 768), BF),
            pltpu.VMEM((192, 16, TC), BF),
            pltpu.VMEM((6, TR, N), BF),
            pltpu.VMEM((TR, TC), F32),
            pltpu.VMEM((5, TR, TC), BF),
            pltpu.VMEM((6, 96, 768), BF),
            pltpu.VMEM((256, 768), F32),
            pltpu.VMEM((4, 768, 768), BF),
            pltpu.SemaphoreType.DMA((SEMS,)),
        ],
        compiler_params=pltpu.CompilerParams(
            collective_id=0, has_side_effects=True, vmem_limit_bytes=60 * 1024 * 1024
        ),
    )(fock, density, margin, fills, firsts, jnp.swapaxes(seconds, 0, 1), owner_order)


def solution(mesh):
    return jax.shard_map(
        on_device,
        mesh=mesh,
        in_specs=(
            P("row", "col"),
            P("row", "col"),
            P("row", "col"),
            P(None, "row", "col"),
            P(None, "row", "col"),
            P(),
            P(None, "row", "col"),
        ),
        out_specs=P("row", "col"),
        check_vma=False,
    )
```
